256 devices in a mesh: step: 16 (over z_lo, x, core), frame: 4 (over y), strip: 4 (over z_hi).
Axes of the slice: x: 4, y: 4, z: 8 (z_hi: 4, z_lo: 2; z = z_hi * 2 + z_lo), core: 2. Of those that a mesh axis runs over, the one named last changes fastest.
Arguments:
- enc_feats: bfloat16 [320, 8, 32, 128], P('step', 'frame', 'strip'), may hold values from -64 to 64
- skip_feats: bfloat16 [320, 8, 32, 128], P('step', 'frame', 'strip'), may hold values from -64 to 64
- timesteps: int32 [16], P('step'), may hold values from 0 to 999
- time_first: bfloat16 [320, 1280], replicated, may hold values from -0.3125 to 0.3125
- time_second: bfloat16 [1280, 1280], replicated, may hold values from -0.15625 to 0.15625
- embed_proj: bfloat16 [1280, 320], replicated, may hold values from -0.15625 to 0.15625
- conv_first: bfloat16 [3, 3, 320, 640], replicated, may hold values from -0.078125 to 0.078125
- conv_second: bfloat16 [3, 3, 320, 320], replicated, may hold values from -0.109375 to 0.109375
- temporal_weight: bfloat16 [3, 320, 320], replicated, may hold values from -0.1875 to 0.1875
- skip_weight: bfloat16 [320, 640], replicated, may hold values from -0.25 to 0.25
Outputs:
- decoded: bfloat16 [16, 320, 8, 32, 128], P('step', None, 'frame', 'strip')
The draws below stay inside these ranges and needn't reach their ends.
All inputs are finite; a program needn't handle non-finite values.
Results may differ from the reference program's by a relative error of at most 0.0035.
Values may be sent and summed in bfloat16 or wider, within the bound.
No kernel may reach another device: no remote copies, remote signals or barrier semaphores. Data moves between devices by JAX's collectives and lax.ppermute only.
A program may use at most 64 MiB of HBM per device.

```python
import math
import jax
import jax.numpy as jnp
from jax import lax

C = 320
GROUPS = 32
COLS = 128
TEMB = 1280
STEPS = 16
FRAMES = 8
ROWS = 32


def feature_field(key, salt):
    key = jax.random.fold_in(key, salt)
    key_chan, key_rough, key_main = jax.random.split(key, 3)
    frame_pos = jnp.arange(FRAMES, dtype=jnp.float32) / max(FRAMES - 1, 1)
    row_pos = jnp.arange(ROWS, dtype=jnp.float32) / max(ROWS - 1, 1)
    chan_pos = jax.random.uniform(key_chan, (C,), jnp.float32)
    rough_rows = jnp.exp(jax.random.uniform(key_rough, (FRAMES, ROWS), jnp.float32, math.log(0.6), math.log(1.6)))
    level_rows = 0.5 * (frame_pos[:, None] + row_pos[None, :])
    scale_field = jnp.exp(math.log(10.0) * (level_rows[None, :, :] + chan_pos[:, None, None] - 1.0)) * rough_rows[None, :, :]
    noise_field = jax.random.normal(key_main, (C, FRAMES, ROWS, COLS), jnp.float32)
    noise_field = jnp.clip(noise_field, -4.0, 4.0)
    return (scale_field[:, :, :, None] * noise_field).astype(jnp.bfloat16)


def draw_enc_feats(key, part):
    return feature_field(key, 11)


def draw_skip_feats(key, part):
    return feature_field(key, 23)


def with_ends(result, key, low, high):
    dims = result.shape
    index_at = [jax.random.randint(jax.random.fold_in(key, axis), (), 0, dims[axis]) for axis in range(len(dims))]
    result = result.at[tuple(index_at)].set(low)
    longest = dims.index(max(dims))
    index_at[longest] = (index_at[longest] + 1) % dims[longest]
    return result.at[tuple(index_at)].set(high)


def scatter_about(rng, extent, width, most, held_as=jnp.bfloat16):
    return jnp.clip(width * jax.random.normal(rng, extent, jnp.float32), -most, most).astype(held_as)


def setup_inputs(seed: int = 0) -> dict:
    seeds = jax.random.split(jax.random.key(seed), 11)
    enc_feats = draw_enc_feats(jax.random.fold_in(seeds[10], 71), 0)
    skip_feats = draw_skip_feats(jax.random.fold_in(seeds[10], 71), 0)
    timesteps = with_ends(jax.random.randint(seeds[2], (STEPS,), 0, 1000), jax.random.fold_in(seeds[2], 1), 0, 999).astype(jnp.int32)
    time_first = scatter_about(seeds[3], (C, TEMB), C ** -0.5, 0.3125)
    time_second = scatter_about(seeds[4], (TEMB, TEMB), TEMB ** -0.5, 0.15625)
    embed_proj = scatter_about(seeds[5], (TEMB, C), TEMB ** -0.5, 0.15625)
    conv_first = scatter_about(seeds[6], (3, 3, C, 2 * C), (18 * C) ** -0.5, 0.078125)
    conv_second = scatter_about(seeds[7], (3, 3, C, C), (9 * C) ** -0.5, 0.109375)
    temporal_weight = scatter_about(seeds[8], (3, C, C), (3 * C) ** -0.5, 0.1875)
    skip_weight = scatter_about(seeds[9], (C, 2 * C), (2 * C) ** -0.5, 0.25)
    return {"enc_feats": enc_feats, "skip_feats": skip_feats, "timesteps": timesteps, "time_first": time_first, "time_second": time_second, "embed_proj": embed_proj, "conv_first": conv_first, "conv_second": conv_second, "temporal_weight": temporal_weight, "skip_weight": skip_weight}


norm_eps = 1e-05

def conv_taps(padded, weights):
    row_count = padded.shape[2] - 2
    col_count = padded.shape[3]
    padded_cols = jnp.pad(padded.astype(jnp.float32), ((0, 0), (0, 0), (0, 0), (1, 1)))
    running = jnp.zeros((weights.shape[2], padded.shape[1], row_count, col_count), jnp.float32)
    for row_off in range(3):
        for col_off in range(3):
            tap_weight = weights[row_off, col_off].astype(jnp.float32)
            window = padded_cols[:, :, row_off:row_off + row_count, col_off:col_off + col_count]
            running = running + jnp.einsum('oi,ifhw->ofhw', tap_weight, window)
    return running

def group_silu(values, groups):
    per_group = values.shape[0] // groups
    count_all = values.shape[1] * values.shape[2] * values.shape[3] * per_group
    sum_one = lax.optimization_barrier(jnp.sum(values, axis=(1, 2, 3)))
    sum_two = lax.optimization_barrier(jnp.sum(values * values, axis=(1, 2, 3)))
    mean_group = sum_one.reshape(groups, per_group).sum(axis=1) / count_all
    square_group = sum_two.reshape(groups, per_group).sum(axis=1) / count_all
    rstd_group = lax.rsqrt(square_group - mean_group * mean_group + norm_eps)
    mean_chan = jnp.repeat(mean_group, per_group)
    rstd_chan = jnp.repeat(rstd_group, per_group)
    return jax.nn.silu((values - mean_chan[:, None, None, None]) * rstd_chan[:, None, None, None])

def reference(enc_feats, skip_feats, timesteps, time_first, time_second, embed_proj, conv_first, conv_second, temporal_weight, skip_weight):
    joined = jnp.concatenate([enc_feats, skip_feats], axis=0)
    act_in = group_silu(joined.astype(jnp.float32), GROUPS).astype(jnp.bfloat16)
    conv_out = conv_taps(jnp.pad(act_in, ((0, 0), (0, 0), (1, 1), (0, 0))), conv_first)
    skip_out = jnp.einsum('oi,ifhw->ofhw', skip_weight.astype(jnp.float32), joined.astype(jnp.float32))
    half_chans = C // 2
    freq_table = jnp.exp(-math.log(10000.0) * jnp.arange(half_chans, dtype=jnp.float32) / half_chans)
    angle_rows = timesteps.astype(jnp.float32)[:, None] * freq_table[None, :]
    sinus_rows = jnp.concatenate([jnp.cos(angle_rows), jnp.sin(angle_rows)], axis=1).astype(jnp.bfloat16)
    embed_one = jax.nn.silu(jnp.dot(sinus_rows, time_first, preferred_element_type=jnp.float32)).astype(jnp.bfloat16)
    embed_two = jax.nn.silu(jnp.dot(embed_one, time_second, preferred_element_type=jnp.float32)).astype(jnp.bfloat16)
    step_embed = jnp.dot(embed_two, embed_proj, preferred_element_type=jnp.float32)

    def one_step(embed_row):
        hidden = conv_out + embed_row[:, None, None, None]
        mid_act = group_silu(hidden, GROUPS).astype(jnp.bfloat16)
        second = conv_taps(jnp.pad(mid_act, ((0, 0), (0, 0), (1, 1), (0, 0))), conv_second)
        temporal_in = jax.nn.silu(second).astype(jnp.bfloat16)
        framed = jnp.pad(temporal_in, ((0, 0), (1, 1), (0, 0), (0, 0))).astype(jnp.float32)
        frame_count = second.shape[1]
        mixed_out = second
        for offset in range(3):
            mixed_out = mixed_out + jnp.einsum('oi,ifhw->ofhw', temporal_weight[offset].astype(jnp.float32), framed[:, offset:offset + frame_count])
        return (skip_out + mixed_out).astype(jnp.bfloat16)
    return lax.map(one_step, step_embed)
```

```python
import math

import jax
import jax.numpy as jnp
from jax import lax
from jax.sharding import PartitionSpec as P

GROUPS = 32


norm_eps = 1e-05


def with_halo(cells, sides, width):
    for axis, dim in sides:
        count = lax.axis_size(axis)
        ends = count - 1
        head = lax.slice_in_dim(cells, 0, width, axis=dim)
        tail = lax.slice_in_dim(cells, cells.shape[dim] - width, cells.shape[dim], axis=dim)
        cells = jnp.concatenate(
            [
                lax.ppermute(tail, axis, [(i, (i + 1) % count) for i in range(ends)]),
                cells,
                lax.ppermute(head, axis, [((i + 1) % count, i) for i in range(ends)]),
            ],
            axis=dim,
        )
    return cells


def conv_taps(padded, weights):
    row_count = padded.shape[2] - 2
    col_count = padded.shape[3]
    padded_cols = jnp.pad(padded, ((0, 0), (0, 0), (0, 0), (1, 1)))
    running = jnp.zeros((weights.shape[2], padded.shape[1], row_count, col_count), jnp.float32)
    for row_off in range(3):
        for col_off in range(3):
            window = padded_cols[:, :, row_off : row_off + row_count, col_off : col_off + col_count]
            running = running + jnp.einsum(
                "oi,ifhw->ofhw",
                weights[row_off, col_off],
                window,
                preferred_element_type=jnp.float32,
            )
    return running


def sum_over(values, axis):
    count = lax.axis_size(axis)
    moved = [
        lax.ppermute(values, axis, [(i, (i + k) % count) for i in range(count)])
        for k in range(1, count)
    ]
    total = values
    for piece in moved:
        total = total + piece
    return total


def sum_over_step(values):
    count = lax.axis_size("step")
    reach = 1
    while reach < count:
        values = values + lax.ppermute(values, "step", [(i, i ^ reach) for i in range(count)])
        reach *= 2
    return values


def channel_scales(sum_one, sum_two, groups, count_all):
    per_group = sum_one.shape[0] // groups
    mean_group = sum_one.reshape(groups, per_group).sum(axis=1) / count_all
    square_group = sum_two.reshape(groups, per_group).sum(axis=1) / count_all
    rstd_group = lax.rsqrt(square_group - mean_group * mean_group + norm_eps)
    return (jnp.repeat(mean_group, per_group), jnp.repeat(rstd_group, per_group))


def on_device(
    enc_feats,
    skip_feats,
    timesteps,
    time_first,
    time_second,
    embed_proj,
    conv_first,
    conv_second,
    temporal_weight,
    skip_weight,
):
    channels = conv_second.shape[2]
    own_chans = enc_feats.shape[0]
    frames = enc_feats.shape[1]
    row_count = enc_feats.shape[2]
    col_count = enc_feats.shape[3]
    spread = lax.axis_size("frame") * lax.axis_size("strip")
    chan_start = lax.axis_index("step") * own_chans
    stacked = jnp.stack([enc_feats, skip_feats])
    wide_feats = stacked.astype(jnp.float32)
    local_one = jnp.sum(wide_feats, axis=(2, 3, 4))
    local_two = jnp.sum(wide_feats * wide_feats, axis=(2, 3, 4))
    anchor = jnp.zeros((), jnp.int32)
    place_one = lax.dynamic_update_slice(
        jnp.zeros((2, channels), jnp.float32), local_one, (anchor, chan_start)
    )
    place_two = lax.dynamic_update_slice(
        jnp.zeros((2, channels), jnp.float32), local_two, (anchor, chan_start)
    )
    packed = jnp.stack([place_one, place_two])
    packed = sum_over(sum_over(packed, "frame"), "strip")
    packed = packed.reshape(2 * 2, channels)
    gathered = sum_over_step(packed)
    total_one, total_two = gathered[:2], gathered[2:]
    in_count = frames * row_count * col_count * spread * (2 * channels // GROUPS)
    mean_in, rstd_in = channel_scales(
        total_one.reshape(-1), total_two.reshape(-1), GROUPS, in_count
    )
    rimmed = with_halo(stacked, (("strip", 3),), 1)
    strip_at = lax.axis_index("strip")
    strip_last = lax.axis_size("strip") - 1
    positions = jnp.arange(row_count + 2)
    row_keep = (
        ((positions > 0) | (strip_at > 0)) & ((positions < row_count + 1) | (strip_at < strip_last))
    ).astype(jnp.float32)
    pieces = lax.all_gather(rimmed, "step", axis=1, tiled=True)
    chans_here = pieces.shape[1]
    mean_rows = jnp.stack(
        [
            lax.slice_in_dim(mean_in, 0, chans_here, axis=0),
            lax.dynamic_slice_in_dim(mean_in, channels, chans_here),
        ]
    )
    rstd_rows = jnp.stack(
        [
            lax.slice_in_dim(rstd_in, 0, chans_here, axis=0),
            lax.dynamic_slice_in_dim(rstd_in, channels, chans_here),
        ]
    )
    normed = jax.nn.silu(
        (pieces.astype(jnp.float32) - mean_rows[:, :, None, None, None])
        * rstd_rows[:, :, None, None, None]
    )
    normed = normed * row_keep[None, None, None, :, None]
    act_rows = normed.astype(jnp.bfloat16).reshape(2 * chans_here, frames, row_count + 2, col_count)
    tap_weights = jnp.concatenate(
        [
            lax.slice_in_dim(conv_first, 0, chans_here, axis=3),
            lax.dynamic_slice_in_dim(conv_first, channels, chans_here, 3),
        ],
        axis=3,
    )
    skip_cols = jnp.concatenate(
        [
            lax.slice_in_dim(skip_weight, 0, chans_here, axis=1),
            lax.dynamic_slice_in_dim(skip_weight, channels, chans_here, 1),
        ],
        axis=1,
    )
    inner_rows = pieces[:, :, :, 1 : row_count + 1].reshape(
        2 * chans_here, frames, row_count, col_count
    )
    conv_part = conv_taps(act_rows, tap_weights)
    skip_part = jnp.einsum(
        "oi,ifhw->ofhw", skip_cols, inner_rows, preferred_element_type=jnp.float32
    )
    half_chans = channels // 2
    freq_table = jnp.exp(
        -math.log(10000.0) * jnp.arange(half_chans, dtype=jnp.float32) / half_chans
    )
    angle_rows = timesteps.astype(jnp.float32)[:, None] * freq_table[None, :]
    sinus_rows = jnp.concatenate([jnp.cos(angle_rows), jnp.sin(angle_rows)], axis=1).astype(
        jnp.bfloat16
    )
    embed_one = jax.nn.silu(
        jnp.dot(sinus_rows, time_first, preferred_element_type=jnp.float32)
    ).astype(jnp.bfloat16)
    embed_two = jax.nn.silu(
        jnp.dot(embed_one, time_second, preferred_element_type=jnp.float32)
    ).astype(jnp.bfloat16)
    step_embed = jnp.dot(embed_two, embed_proj, preferred_element_type=jnp.float32)
    hidden = conv_part + step_embed[0][:, None, None, None]
    hidden_one = jnp.sum(hidden, axis=(1, 2, 3))
    hidden_two = jnp.sum(hidden * hidden, axis=(1, 2, 3))
    packed_mid = jnp.stack([hidden_one, hidden_two])
    packed_mid = sum_over(sum_over(packed_mid, "frame"), "strip")
    total_hone, total_htwo = packed_mid[0], packed_mid[1]
    mid_count = frames * row_count * col_count * spread * (channels // GROUPS)
    mean_mid, rstd_mid = channel_scales(total_hone, total_htwo, GROUPS, mid_count)
    mid_act = jax.nn.silu(
        (hidden - mean_mid[:, None, None, None]) * rstd_mid[:, None, None, None]
    ).astype(jnp.bfloat16)
    mid_rim = with_halo(mid_act, (("strip", 2),), 1)
    second = conv_taps(mid_rim, conv_second)
    temporal_in = jax.nn.silu(second).astype(jnp.bfloat16)
    framed = with_halo(temporal_in, (("frame", 1),), 1)
    mixed_out = second
    for offset in range(3):
        mixed_out = mixed_out + jnp.einsum(
            "oi,ifhw->ofhw",
            temporal_weight[offset],
            framed[:, offset : offset + frames],
            preferred_element_type=jnp.float32,
        )
    decoded = (skip_part + mixed_out).astype(jnp.bfloat16)
    return decoded[None]


def solution(mesh):
    return jax.shard_map(
        on_device,
        mesh=mesh,
        in_specs=(
            P("step", "frame", "strip", None),
            P("step", "frame", "strip", None),
            P("step"),
            P(),
            P(),
            P(),
            P(),
            P(),
            P(),
            P(),
        ),
        out_specs=P("step", None, "frame", "strip", None),
        check_vma=False,
    )
```

```python
import functools
import math

import jax
import jax.numpy as jnp
from jax import lax
from jax.experimental import pallas as pl
from jax.experimental.pallas import tpu as pltpu
from jax.sharding import PartitionSpec as P

GROUPS = 32

norm_eps = 1e-05


IN_VMEM = pl.BlockSpec(memory_space=pltpu.VMEM)
IN_SMEM = pl.BlockSpec(memory_space=pltpu.SMEM)


def core_swap(values):
    return lax.ppermute(values, "step", [(i, i ^ 1) for i in range(16)])


def z_swap(values):
    return lax.ppermute(values, "step", [(i, i ^ 8) for i in range(16)])


def step_index(z, x, core):
    return z * 8 + x % 4 * 2 + core


def from_x(values, shift):
    shifts = shift if isinstance(shift, tuple) else (shift, shift)
    pairs = [
        (step_index(z, x + shifts[core], core), step_index(z, x, core))
        for z in range(2)
        for x in range(4)
        for core in range(2)
    ]
    return lax.ppermute(values, "step", pairs)


def to_frames(values, shifts):
    count = lax.axis_size("frame")
    pairs = []
    for step in range(16):
        for frame in range(count):
            target = frame + shifts[step % 2]
            if 0 <= target < count:
                pairs.append((step * count + frame, step * count + target))
    return lax.ppermute(values, ("step", "frame"), pairs)


def sum_over(values, axis):
    count = lax.axis_size(axis)
    moved = [
        lax.ppermute(values, axis, [(i, (i + k) % count) for i in range(count)])
        for k in range(1, count)
    ]
    total = values
    for piece in moved:
        total = total + piece
    return total


def edge_rows(first, last):
    count = lax.axis_size("strip")
    before = lax.ppermute(last, "strip", [(i, i + 1) for i in range(count - 1)])
    after = lax.ppermute(first, "strip", [(i + 1, i) for i in range(count - 1)])
    return before, after


def silu(v):
    return v * (0.5 * jnp.tanh(0.5 * v) + 0.5)


def join_columns(acc, half, outs):
    lanes = slice(half * 128, half * 128 + 128)
    lane = lax.broadcasted_iota(jnp.int32, (outs, 128), 1)
    left = pltpu.roll(acc[0:outs, lanes], 1, axis=1)
    right = pltpu.roll(acc[2 * outs : 3 * outs, lanes], 127, axis=1)
    return (
        acc[outs : 2 * outs, lanes]
        + jnp.where(lane == 0, 0.0, left)
        + jnp.where(lane == 127, 0.0, right)
    )


def one_hot(rows, cols, per, by_row):
    row = lax.broadcasted_iota(jnp.int32, (rows, cols), 0)
    col = lax.broadcasted_iota(jnp.int32, (rows, cols), 1)
    low, high = (col * per, row) if by_row else (row * per, col)
    return ((high >= low) & (high < low + per)).astype(jnp.float32)


def exact_dot(a, b):
    return jnp.dot(a, b, precision=lax.Precision.HIGHEST, preferred_element_type=jnp.float32)


def first_weights_kernel(first_ref, out_ref):
    width = first_ref.shape[2]
    for tap in range(3):
        out_ref[:, tap * width : (tap + 1) * width] = first_ref[tap]


def second_weights_kernel(second_ref, temporal_ref, core_ref, out_ref, near_ref):
    width = second_ref.shape[2]
    out_ref[...] = jnp.concatenate([second_ref[0], second_ref[1], second_ref[2]], axis=1)
    side = 2 - 2 * core_ref[0]
    middle = temporal_ref[1]
    near_ref[0:width, :] = jnp.concatenate([middle, temporal_ref[side]], axis=1)
    near_ref[width : 2 * width, :] = jnp.concatenate([temporal_ref[2 - side], middle], axis=1)


def first_kernel(
    place_ref, keep_ref, own_ref, z_ref, a_ref, b_ref, az_ref, bz_ref, d_ref, dz_ref,
    scale_ref, weight_ref, skip_weight_ref, embed_ref,
    conv_ref, skip_ref, sums_ref,
    act_ref, plain_ref, wide_ref, raw_ref, total_ref, scales_ref,
):
    chans = act_ref.shape[1]
    per = own_ref.shape[1] // 2
    rows = conv_ref.shape[0]
    outs = conv_ref.shape[1]
    spread = one_hot(chans, GROUPS, chans // GROUPS, True)
    scales_ref[0] = exact_dot(spread, scale_ref[0])
    scales_ref[1] = exact_dot(spread, scale_ref[1])
    refs = (own_ref, z_ref, a_ref, b_ref, az_ref, bz_ref, d_ref, dz_ref)
    for slot, ref in enumerate(refs):
        for kind in range(2):
            at = pl.multiple_of(place_ref[slot] * per, 8) + kind * (chans // 2)
            at = pl.multiple_of(at, 8)
            mean = scales_ref[0, pl.ds(at, per), :]
            rstd = scales_ref[1, pl.ds(at, per), :]
            for row in range(rows + 2):
                raw = ref[row, kind * per : (kind + 1) * per, :].astype(jnp.float32)
                act = silu((raw - mean) * rstd)
                if row == 0:
                    act = act * keep_ref[0]
                if row == rows + 1:
                    act = act * keep_ref[1]
                act_ref[row, pl.ds(at, per), :] = act
                if 0 < row < rows + 1:
                    plain_ref[row - 1, pl.ds(at, per), :] = raw
    for row in range(rows + 2):
        act = act_ref[row].astype(jnp.bfloat16)
        if row < rows + 1:
            wide_ref[row * chans : (row + 1) * chans, 0:128] = act
        if row > 0:
            wide_ref[(row - 1) * chans : row * chans, 128:256] = act
    for row in range(rows):
        lanes = slice(row % 2 * 128, row % 2 * 128 + 128)
        pair = row // 2
        raw_ref[pair * chans : (pair + 1) * chans, lanes] = plain_ref[row].astype(jnp.bfloat16)
    total_ref[...] = jnp.zeros_like(total_ref)
    for pair in range(rows // 2):
        acc = jnp.dot(
            weight_ref[...],
            wide_ref[2 * pair * chans : (2 * pair + 3) * chans, :],
            preferred_element_type=jnp.float32,
        )
        skip = jnp.dot(
            skip_weight_ref[...],
            raw_ref[pair * chans : (pair + 1) * chans, :],
            preferred_element_type=jnp.float32,
        ).astype(jnp.bfloat16)
        for half in range(2):
            row = 2 * pair + half
            out = join_columns(acc, half, outs)
            conv_ref[row] = out.astype(jnp.bfloat16)
            skip_ref[row] = skip[:, half * 128 : half * 128 + 128]
            for who in range(2):
                hidden = out + embed_ref[who]
                total_ref[2 * who] += hidden
                total_ref[2 * who + 1] += hidden * hidden
    gather = one_hot(GROUPS, outs, outs // GROUPS, False)
    for which in range(4):
        sums_ref[which // 2, which % 2] = exact_dot(gather, total_ref[which])


def second_kernel(
    keep_ref, conv_ref, before_ref, after_ref, sums_ref, embed_ref, weight_ref,
    second_ref, temporal_ref, wide_ref, *, count_all,
):
    rows, chans = conv_ref.shape[0], conv_ref.shape[1]
    mean = jnp.sum(sums_ref[0], axis=1, keepdims=True) / count_all
    square = jnp.sum(sums_ref[1], axis=1, keepdims=True) / count_all
    scale = lax.rsqrt(square - mean * mean + norm_eps)
    spread = one_hot(chans, GROUPS, chans // GROUPS, True)
    lanes = (GROUPS, 128)
    shift = embed_ref[0] - exact_dot(spread, jnp.broadcast_to(mean, lanes))
    rstd = exact_dot(spread, jnp.broadcast_to(scale, lanes))
    for row in range(rows + 2):
        if row == 0:
            raw = before_ref[...]
        elif row == rows + 1:
            raw = after_ref[...]
        else:
            raw = conv_ref[row - 1]
        act = silu((raw.astype(jnp.float32) + shift) * rstd)
        if row == 0:
            act = act * keep_ref[0]
        if row == rows + 1:
            act = act * keep_ref[1]
        act = act.astype(jnp.bfloat16)
        if row < rows + 1:
            wide_ref[row * chans : (row + 1) * chans, 0:128] = act
        if row > 0:
            wide_ref[(row - 1) * chans : row * chans, 128:256] = act
    for pair in range(rows // 2):
        acc = jnp.dot(
            weight_ref[...],
            wide_ref[2 * pair * chans : (2 * pair + 3) * chans, :],
            preferred_element_type=jnp.float32,
        )
        for half in range(2):
            row = 2 * pair + half
            out = join_columns(acc, half, chans)
            second_ref[row] = out
            temporal_ref[row] = silu(out).astype(jnp.bfloat16)


def near_kernel(t0_ref, t1_ref, s0_ref, s1_ref, k0_ref, k1_ref, weight_ref, out_ref):
    rows, chans = t0_ref.shape[0], t0_ref.shape[1]
    for pair in range(rows // 2):
        a, b = 2 * pair, 2 * pair + 1
        both = jnp.concatenate(
            [
                jnp.concatenate([t0_ref[a], t0_ref[b]], axis=1),
                jnp.concatenate([t1_ref[a], t1_ref[b]], axis=1),
            ],
            axis=0,
        )
        acc = jnp.dot(weight_ref[...], both, preferred_element_type=jnp.float32)
        for half in range(2):
            row = 2 * pair + half
            lanes = slice(half * 128, half * 128 + 128)
            out_ref[0, row] = acc[0:chans, lanes] + s0_ref[row] + k0_ref[row].astype(jnp.float32)
            out_ref[1, row] = acc[chans:, lanes] + s1_ref[row] + k1_ref[row].astype(jnp.float32)


def far_kernel(core_ref, own_side_ref, other_side_ref, base_ref, weight_ref, out_ref):
    rows, chans = own_side_ref.shape[0], own_side_ref.shape[1]
    core = core_ref[0]
    sides = ((own_side_ref, 2 * core, core), (other_side_ref, 2 - 2 * core, 1 - core))
    for which, (ref, tap, frame) in enumerate(sides):
        weight = weight_ref[tap]
        lines = []
        for pair in range(rows // 2):
            side = jnp.concatenate([ref[2 * pair], ref[2 * pair + 1]], axis=1)
            acc = jnp.dot(weight, side, preferred_element_type=jnp.float32)
            for half in range(2):
                row = 2 * pair + half
                lanes = slice(half * 128, half * 128 + 128)
                lines.append(acc[:, lanes] + base_ref[which, row])
        block = jnp.transpose(jnp.stack(lines), (1, 0, 2)).astype(jnp.bfloat16)
        out_ref[:, pl.ds(frame, 1), :, :] = block[:, None]


def kernel_call(body, name, outs, smem, *args, scratch=(), limit=16):
    specs = [IN_SMEM if i in smem else IN_VMEM for i in range(len(args))]
    return pl.pallas_call(
        body,
        name=name,
        out_shape=outs,
        in_specs=specs,
        out_specs=jax.tree.map(lambda _: IN_VMEM, outs),
        scratch_shapes=list(scratch),
        compiler_params=pltpu.CompilerParams(vmem_limit_bytes=limit << 20),
    )(*args)


def group_scales(sum_one, sum_two, count_all):
    mean_group = sum_one / count_all
    square_group = sum_two / count_all
    return mean_group, lax.rsqrt(square_group - mean_group * mean_group + norm_eps)


def on_device(
    enc_feats, skip_feats, timesteps, time_first, time_second, embed_proj,
    conv_first, conv_second, temporal_weight, skip_weight,
):
    channels = conv_second.shape[2]
    own_chans, frames, rows, cols = enc_feats.shape
    spread = lax.axis_size("frame") * lax.axis_size("strip")
    step_at = lax.axis_index("step")
    core, x_at, z_at = step_at % 2, (step_at // 2) % 4, step_at // 8
    strip_at = lax.axis_index("strip")
    keep = jnp.stack([strip_at > 0, strip_at < lax.axis_size("strip") - 1]).astype(jnp.float32)
    per_group = 2 * channels // GROUPS

    joined = jnp.stack([enc_feats, skip_feats])
    planes = jnp.transpose(joined, (2, 3, 0, 1, 4))
    kept = lax.dynamic_index_in_dim(planes, core, 0, keepdims=False)
    given = lax.dynamic_index_in_dim(planes, 1 - core, 0, keepdims=False)
    taken = core_swap(given)
    chunk = jnp.concatenate(
        [jnp.where(core == 0, kept, taken), jnp.where(core == 0, taken, kept)], axis=2
    ).reshape(rows, 4 * own_chans, cols)
    before, after = edge_rows(chunk[:1], chunk[rows - 1 :])
    own = jnp.concatenate([before, chunk, after], axis=0)

    ahead, behind = (1, -1), (-1, 1)
    z_piece = z_swap(own)
    a_piece = from_x(own, ahead)
    b_piece = from_x(own, behind)
    az_piece = from_x(z_piece, ahead)
    bz_piece = from_x(z_piece, behind)
    d_piece = from_x(a_piece, ahead)
    dz_piece = from_x(bz_piece, behind)
    other = 1 - z_at
    turn = 1 - 2 * core
    right, left, far = (x_at + turn + 4) % 4, (x_at - turn + 4) % 4, (x_at + 2) % 4
    place = jnp.stack(
        [
            z_at * 4 + x_at,
            other * 4 + x_at,
            z_at * 4 + right,
            z_at * 4 + left,
            other * 4 + right,
            other * 4 + left,
            z_at * 4 + far,
            other * 4 + far,
        ]
    ).astype(jnp.int32)

    wide = joined.astype(jnp.float32)
    local = jnp.stack([jnp.sum(wide, axis=(1, 2, 3, 4)), jnp.sum(wide * wide, axis=(1, 2, 3, 4))])
    total = sum_over(sum_over(local, "frame"), "strip")
    in_count = frames * rows * cols * spread * per_group
    mean_own, rstd_own = group_scales(total[0], total[1], in_count)
    scales_own = jnp.stack([mean_own, rstd_own])
    slots = lax.dynamic_update_slice(
        jnp.zeros((2, 2, 16), jnp.float32), scales_own[:, :, None], (0, 0, step_at)
    )
    slots = slots + core_swap(slots)
    slots = slots + z_swap(slots)
    slots = slots + from_x(slots, 1) + from_x(slots, 2) + from_x(slots, 3)
    scales = jnp.broadcast_to(slots.reshape(2, GROUPS, 1), (2, GROUPS, cols))

    width = 2 * channels
    core_word = core.astype(jnp.int32)[None]
    first_weight = kernel_call(
        first_weights_kernel,
        "first_weights",
        jax.ShapeDtypeStruct((3 * channels, 3 * width), jnp.bfloat16),
        (),
        conv_first.reshape(3, 3 * channels, width),
    )
    second_weight, near_weight = kernel_call(
        second_weights_kernel,
        "second_weights",
        (
            jax.ShapeDtypeStruct((3 * channels, 3 * channels), jnp.bfloat16),
            jax.ShapeDtypeStruct((2 * channels, 2 * channels), jnp.bfloat16),
        ),
        (2,),
        conv_second.reshape(3, 3 * channels, channels),
        temporal_weight,
        core_word,
    )

    half_chans = channels // 2
    freq_table = jnp.exp(
        -math.log(10000.0) * jnp.arange(half_chans, dtype=jnp.float32) / half_chans
    )
    angle_rows = timesteps.astype(jnp.float32)[:, None] * freq_table[None, :]
    sinus_rows = jnp.concatenate([jnp.cos(angle_rows), jnp.sin(angle_rows)], axis=1).astype(
        jnp.bfloat16
    )
    embed_one = jax.nn.silu(
        jnp.dot(sinus_rows, time_first, preferred_element_type=jnp.float32)
    ).astype(jnp.bfloat16)
    embed_two = jax.nn.silu(
        jnp.dot(embed_one, time_second, preferred_element_type=jnp.float32)
    ).astype(jnp.bfloat16)
    embed = jnp.dot(embed_two, embed_proj, preferred_element_type=jnp.float32)[0]
    embeds = jnp.stack([embed, core_swap(embed)])
    embed_wide = jnp.broadcast_to(embeds[:, :, None], (2, channels, cols))

    bf16_rows = jax.ShapeDtypeStruct((rows, channels, cols), jnp.bfloat16)
    f32_rows = jax.ShapeDtypeStruct((rows, channels, cols), jnp.float32)
    conv_own, side_own, sums = kernel_call(
        first_kernel,
        "first_conv",
        (bf16_rows, bf16_rows, jax.ShapeDtypeStruct((2, 2, GROUPS, cols), jnp.float32)),
        (0, 1),
        place, keep, own, z_piece, a_piece, b_piece, az_piece, bz_piece, d_piece, dz_piece,
        scales, first_weight, skip_weight, embed_wide,
        scratch=(
            pltpu.VMEM((rows + 2, width, cols), jnp.float32),
            pltpu.VMEM((rows, width, cols), jnp.float32),
            pltpu.VMEM(((rows + 1) * width, 256), jnp.bfloat16),
            pltpu.VMEM((rows // 2 * width, 256), jnp.bfloat16),
            pltpu.VMEM((4, channels, cols), jnp.float32),
            pltpu.VMEM((2, width, cols), jnp.float32),
        ),
        limit=24,
    )

    mine = sums[0] + core_swap(sums[1])
    mine = sum_over(sum_over(mine, "frame"), "strip")
    mid_count = frames * rows * cols * spread * (channels // GROUPS)

    up, down = edge_rows(conv_own[0], conv_own[rows - 1])
    conv_other = core_swap(conv_own)
    side_other = core_swap(side_own)
    rims_other = core_swap(jnp.stack([up, down]))

    def second_conv(conv, up, down, name):
        return kernel_call(
            functools.partial(second_kernel, count_all=mid_count),
            name,
            (f32_rows, bf16_rows),
            (0,),
            keep, conv, up, down, mine, embed_wide, second_weight,
            scratch=(pltpu.VMEM(((rows + 1) * channels, 256), jnp.bfloat16),),
        )

    second_own, temporal_own = second_conv(conv_own, up, down, "second_own")
    other_side = to_frames(temporal_own, (-1, 1))
    second_other, temporal_other = second_conv(
        conv_other, rims_other[0], rims_other[1], "second_other"
    )
    own_side = to_frames(temporal_other, (1, -1))
    base = kernel_call(
        near_kernel,
        "near",
        jax.ShapeDtypeStruct((2, rows, channels, cols), jnp.float32),
        (),
        temporal_own, temporal_other, second_own, second_other, side_own, side_other, near_weight,
    )
    decoded = kernel_call(
        far_kernel,
        "far",
        jax.ShapeDtypeStruct((channels, 2, rows, cols), jnp.bfloat16),
        (0,),
        core_word, own_side, other_side, base, temporal_weight,
    )
    return decoded[None]


def solution(mesh):
    return jax.shard_map(
        on_device,
        mesh=mesh,
        in_specs=(
            P("step", "frame", "strip", None),
            P("step", "frame", "strip", None),
            P("step"),
            P(),
            P(),
            P(),
            P(),
            P(),
            P(),
            P(),
        ),
        out_specs=P("step", None, "frame", "strip", None),
        check_vma=False,
    )
```

```python
import functools
import math

import jax
import jax.numpy as jnp
from jax import lax
from jax.experimental import pallas as pl
from jax.experimental.pallas import tpu as pltpu
from jax.sharding import PartitionSpec as P


GROUPS = 32

norm_eps = 1e-05


IN_VMEM = pl.BlockSpec(memory_space=pltpu.VMEM)
IN_HBM = pl.BlockSpec(memory_space=pltpu.HBM)
IN_SMEM = pl.BlockSpec(memory_space=pltpu.SMEM)


def step_index(z, x, core):
    return z * 8 + x % 4 * 2 + core


def core_swap(values):
    return lax.ppermute(values, "step", [(i, i ^ 1) for i in range(16)])


def z_swap(values):
    return lax.ppermute(values, "step", [(i, i ^ 8) for i in range(16)])


def from_x(values, shifts):
    pairs = [
        (step_index(z, x + shifts[core], core), step_index(z, x, core))
        for z in range(2)
        for x in range(4)
        for core in range(2)
    ]
    return lax.ppermute(values, "step", pairs)


def to_frames(values, shifts):
    count = lax.axis_size("frame")
    pairs = []
    for step in range(16):
        for frame in range(count):
            target = frame + shifts[step % 2]
            if 0 <= target < count:
                pairs.append((step * count + frame, step * count + target))
    return lax.ppermute(values, ("step", "frame"), pairs)


def to_next_group(values):
    count = lax.axis_size("frame")
    pairs = []
    for step in range(16):
        for frame in range(count):
            target = frame + (-1, 1)[step % 2]
            if 0 <= target < count:
                pairs.append((step * count + frame, (step ^ 1) * count + target))
    return lax.ppermute(values, ("step", "frame"), pairs)


def sum_over(values, axis):
    count = lax.axis_size(axis)
    total = values
    for k in range(1, count):
        total = total + lax.ppermute(values, axis, [(i, (i + k) % count) for i in range(count)])
    return total


def link_swap(values):
    count = lax.axis_size("strip")
    pairs = []
    for step in range(16):
        for strip in range(count):
            beside = (strip + 1 if step >= 8 else strip - 1) % count
            pairs.append((step * count + strip, (step ^ 8) * count + beside))
    return lax.ppermute(values, ("step", "strip"), pairs)


def sum_over_strips(values):
    values = values + lax.ppermute(values, "strip", [(0, 1), (1, 0), (2, 3), (3, 2)])
    return values + lax.ppermute(values, "strip", [(1, 2), (2, 1), (3, 0), (0, 3)])


def edge_rows(first, last, even):
    one = lax.ppermute(jnp.where(even, last, first), "strip", [(0, 1), (1, 0), (2, 3), (3, 2)])
    two = lax.ppermute(jnp.where(even, first, last), "strip", [(1, 2), (2, 1), (3, 0), (0, 3)])
    return jnp.where(even, two, one), jnp.where(even, one, two)


def silu(v):
    return v * (0.5 * jnp.tanh(0.5 * v) + 0.5)


def join_columns(acc, half, outs):
    lanes = slice(half * 128, half * 128 + 128)
    lane = lax.broadcasted_iota(jnp.int32, (outs, 128), 1)
    left = pltpu.roll(acc[0:outs, lanes], 1, axis=1)
    right = pltpu.roll(acc[2 * outs : 3 * outs, lanes], 127, axis=1)
    return (
        acc[outs : 2 * outs, lanes]
        + jnp.where(lane == 0, 0.0, left)
        + jnp.where(lane == 127, 0.0, right)
    )


def one_hot(rows, cols, per, by_row):
    row = lax.broadcasted_iota(jnp.int32, (rows, cols), 0)
    col = lax.broadcasted_iota(jnp.int32, (rows, cols), 1)
    low, high = (col * per, row) if by_row else (row * per, col)
    return ((high >= low) & (high < low + per)).astype(jnp.float32)


def exact_dot(a, b):
    return jnp.dot(a, b, precision=lax.Precision.HIGHEST, preferred_element_type=jnp.float32)


def side_kernel(totals_ref, before_ref, after_ref, out_ref, *, count_all):
    chans = out_ref.shape[1]
    out_ref[0] = before_ref[0]
    out_ref[1] = after_ref[0]
    mean = totals_ref[0] / count_all
    scale = lax.rsqrt(totals_ref[1] / count_all - mean * mean + norm_eps)
    chan = lax.broadcasted_iota(jnp.int32, (chans, 128), 0)
    lane = lax.broadcasted_iota(jnp.int32, (chans, 128), 1)
    per = chans // 4
    plane = jnp.zeros((chans, 128), jnp.float32)
    for which, values in enumerate((mean, scale)):
        wide = jnp.zeros((chans, 128), jnp.float32)
        for group in range(4):
            inside = (chan >= group * per) & (chan < (group + 1) * per)
            wide = jnp.where(inside, values[group : group + 1, :], wide)
        for part in range(3):
            piece = wide.astype(jnp.bfloat16).astype(jnp.float32)
            plane = jnp.where(lane == which * 3 + part, piece, plane)
            wide = wide - piece
    out_ref[2] = plane.astype(jnp.bfloat16)


def second_weights_kernel(second_ref, temporal_ref, core_ref, out_ref, near_ref):
    width = second_ref.shape[2]
    out_ref[...] = jnp.concatenate([second_ref[0], second_ref[1], second_ref[2]], axis=1)
    side = 2 - 2 * core_ref[0]
    middle = temporal_ref[1]
    here, there = temporal_ref[side], temporal_ref[2 - side]
    near_ref[0:width, :] = jnp.concatenate([middle, here, there], axis=1)
    near_ref[width : 2 * width, :] = jnp.concatenate([there, middle, there * 0], axis=1)


def pair_kernel(one_ref, two_ref, out_ref):
    out_ref[0] = one_ref[...]
    out_ref[1] = two_ref[...]


def norm_kernel(step_ref, keep_ref, *refs):
    pieces, sides, (act_ref, plain_ref) = refs[:8], refs[8:12], refs[12:]
    chans = act_ref.shape[1]
    rows = plain_ref.shape[0]
    per = pieces[0].shape[1] // 2
    lane = lax.broadcasted_iota(jnp.int32, (per, 128), 1)
    step = step_ref[0]
    z_at, x_at = step >> 3, step >> 1
    turn = 1 - 2 * (step & 1)
    for slot, ref in enumerate(pieces):
        x_from = (x_at + (0, turn, 4 - turn, 2)[slot // 2]) & 3
        place = (z_at ^ (slot % 2)) * 4 + x_from
        side_ref = sides[slot // 2]
        for kind in range(2):
            here = slice(kind * per, (kind + 1) * per)
            at = pl.multiple_of(place * per, 8) + kind * (chans // 2)
            at = pl.multiple_of(at, 8)
            part = side_ref[slot % 2, 2, here, :].astype(jnp.float32)
            mean = jnp.sum(jnp.where(lane < 3, part, 0.0), axis=1, keepdims=True)
            rstd = jnp.sum(jnp.where((lane >= 3) & (lane < 6), part, 0.0), axis=1, keepdims=True)
            for edge, row in enumerate((0, rows + 1)):
                raw = side_ref[slot % 2, edge, here, :].astype(jnp.float32)
                act_ref[row, pl.ds(at, per), :] = silu((raw - mean) * rstd) * keep_ref[edge]

            def inner(row, carry, ref=ref, here=here, at=at, mean=mean, rstd=rstd):
                raw = ref[row, here, :].astype(jnp.float32)
                act_ref[row + 1, pl.ds(at, per), :] = silu((raw - mean) * rstd)
                plain_ref[row, pl.ds(at, per), :] = raw
                return carry

            lax.fori_loop(0, rows, inner, 0, unroll=2)


def first_kernel(
    act_ref, plain_ref, embed_ref, first_ref, skip_weight_ref,
    conv_ref, skip_ref, sums_ref,
    wide_ref, raw_ref, total_ref, weight_ref, sem,
):
    chans = act_ref.shape[1]
    rows = conv_ref.shape[0]
    outs = conv_ref.shape[1]
    copies = [
        pltpu.make_async_copy(
            first_ref.at[tap], weight_ref.at[:, tap * chans : (tap + 1) * chans], sem.at[tap]
        )
        for tap in range(3)
    ]
    for copy in copies:
        copy.start()
    for row in range(rows + 2):
        act = act_ref[row].astype(jnp.bfloat16)
        if row < rows + 1:
            wide_ref[row * chans : (row + 1) * chans, 0:128] = act
        if row > 0:
            wide_ref[(row - 1) * chans : row * chans, 128:256] = act
    for row in range(rows):
        lanes = slice(row % 2 * 128, row % 2 * 128 + 128)
        pair = row // 2
        raw_ref[pair * chans : (pair + 1) * chans, lanes] = plain_ref[row].astype(jnp.bfloat16)
    total_ref[...] = jnp.zeros_like(total_ref)
    for copy in copies:
        copy.wait()
    for pair in range(rows // 2):
        acc = jnp.dot(
            weight_ref[...],
            wide_ref[2 * pair * chans : (2 * pair + 3) * chans, :],
            preferred_element_type=jnp.float32,
        )
        skip = jnp.dot(
            skip_weight_ref[...],
            raw_ref[pair * chans : (pair + 1) * chans, :],
            preferred_element_type=jnp.float32,
        ).astype(jnp.bfloat16)
        for half in range(2):
            row = 2 * pair + half
            out = join_columns(acc, half, outs)
            conv_ref[row] = out.astype(jnp.bfloat16)
            skip_ref[row] = skip[:, half * 128 : half * 128 + 128]
            for who in range(2):
                hidden = out + embed_ref[who]
                total_ref[2 * who] += hidden
                total_ref[2 * who + 1] += hidden * hidden
    gather = one_hot(GROUPS, outs, outs // GROUPS, False)
    for which in range(4):
        sums_ref[which // 2, which % 2] = exact_dot(gather, total_ref[which])


def second_kernel(
    keep_ref, conv_ref, before_ref, after_ref, sums_ref, embed_ref, weight_ref,
    *outs, count_all,
):
    wide_ref, temporal_ref = outs[-1], outs[-2]
    far = len(outs) == 2
    rows, chans = conv_ref.shape[0], conv_ref.shape[1]
    mean = jnp.sum(sums_ref[0], axis=1, keepdims=True) / count_all
    square = jnp.sum(sums_ref[1], axis=1, keepdims=True) / count_all
    scale = lax.rsqrt(square - mean * mean + norm_eps)
    spread = one_hot(chans, GROUPS, chans // GROUPS, True)
    lanes = (GROUPS, 128)
    shift = embed_ref[0] - exact_dot(spread, jnp.broadcast_to(mean, lanes))
    rstd = exact_dot(spread, jnp.broadcast_to(scale, lanes))
    for row in range(rows + 2):
        if row == 0:
            raw = before_ref[...]
        elif row == rows + 1:
            raw = after_ref[...]
        else:
            raw = conv_ref[row - 1]
        act = silu((raw.astype(jnp.float32) + shift) * rstd)
        if row == 0:
            act = act * keep_ref[0]
        if row == rows + 1:
            act = act * keep_ref[1]
        act = act.astype(jnp.bfloat16)
        if row < rows + 1:
            wide_ref[row * chans : (row + 1) * chans, 0:128] = act
        if row > 0:
            wide_ref[(row - 1) * chans : row * chans, 128:256] = act

    def one_pair(pair, carry):
        at = pl.multiple_of(2 * pair * chans, 16)
        acc = jnp.dot(
            weight_ref[...],
            wide_ref[pl.ds(at, 3 * chans), :],
            preferred_element_type=jnp.float32,
        )
        for half in range(2):
            row = 2 * pair + half
            out = join_columns(acc, half, chans)
            if far:
                temporal_ref[row] = (silu(out) * keep_ref[2]).astype(jnp.bfloat16)
            else:
                outs[0][row] = out
                temporal_ref[row] = silu(out).astype(jnp.bfloat16)
        return carry

    lax.fori_loop(0, rows // 2, one_pair, 0)


def turned(lines):
    return jnp.transpose(jnp.stack(lines), (1, 0, 2)).astype(jnp.bfloat16)


def near_kernel(
    t0_ref, t1_ref, t2_ref, s0_ref, s1_ref, k0_ref, k1_ref, weight_ref, own_ref, base_ref
):
    rows, chans = t0_ref.shape[0], t0_ref.shape[1]
    lines = []
    for pair in range(rows // 2):
        a, b = 2 * pair, 2 * pair + 1
        sides = jnp.concatenate(
            [jnp.concatenate([ref[a], ref[b]], axis=1) for ref in (t0_ref, t1_ref, t2_ref)], axis=0
        )
        acc = jnp.dot(weight_ref[...], sides, preferred_element_type=jnp.float32)
        for half in range(2):
            row = 2 * pair + half
            lanes = slice(half * 128, half * 128 + 128)
            lines.append(acc[0:chans, lanes] + s0_ref[row] + k0_ref[row].astype(jnp.float32))
            base_ref[row] = acc[chans:, lanes] + s1_ref[row] + k1_ref[row].astype(jnp.float32)
    own_ref[...] = turned(lines)


def far_kernel(core_ref, side_ref, base_ref, own_ref, weight_ref, out_ref):
    rows = side_ref.shape[0]
    core = core_ref[0]
    weight = weight_ref[2 - 2 * core]
    out_ref[:, pl.ds(core, 1), :, :] = own_ref[...][:, None]
    lines = []
    for pair in range(rows // 2):
        side = jnp.concatenate([side_ref[2 * pair], side_ref[2 * pair + 1]], axis=1)
        acc = jnp.dot(weight, side, preferred_element_type=jnp.float32)
        for half in range(2):
            lanes = slice(half * 128, half * 128 + 128)
            lines.append(acc[:, lanes] + base_ref[2 * pair + half])
    out_ref[:, pl.ds(1 - core, 1), :, :] = turned(lines)[:, None]


def kernel_call(body, outs, smem, *args, scratch=(), limit=16, hbm=(), work=0):
    specs = [IN_SMEM if i in smem else IN_HBM if i in hbm else IN_VMEM for i in range(len(args))]
    return pl.pallas_call(
        body,
        out_shape=outs,
        in_specs=specs,
        out_specs=jax.tree.map(lambda _: IN_VMEM, outs),
        scratch_shapes=list(scratch),
        cost_estimate=pl.CostEstimate(
            flops=work or 1000000,
            transcendentals=0,
            bytes_accessed=sum(math.prod(a.shape) * a.dtype.itemsize for a in args),
        ),
        compiler_params=pltpu.CompilerParams(vmem_limit_bytes=limit << 20),
    )(*args)


def on_device(
    enc_feats, skip_feats, timesteps, time_first, time_second, embed_proj,
    conv_first, conv_second, temporal_weight, skip_weight,
):
    channels = conv_second.shape[2]
    own_chans, frames, rows, cols = enc_feats.shape
    spread = lax.axis_size("frame") * lax.axis_size("strip")
    step_at = lax.axis_index("step")
    core, z_at = step_at % 2, step_at // 8
    strip_at = lax.axis_index("strip")
    frame_at = lax.axis_index("frame")
    keep = jnp.stack(
        [
            strip_at > 0,
            strip_at < lax.axis_size("strip") - 1,
            jnp.where(core == 0, frame_at > 0, frame_at < lax.axis_size("frame") - 1),
            z_at == 1,
        ]
    ).astype(jnp.float32)
    per_group = 2 * channels // GROUPS

    joined = jnp.stack([enc_feats, skip_feats])
    wide = joined.astype(jnp.float32)
    local = jnp.stack([jnp.sum(wide, axis=(1, 2, 3, 4)), jnp.sum(wide * wide, axis=(1, 2, 3, 4))])

    def by_core(mine, theirs):
        return jnp.where(core == 0, mine, theirs), jnp.where(core == 0, theirs, mine)

    planes = jnp.transpose(joined, (2, 3, 0, 1, 4))
    kept = lax.dynamic_index_in_dim(planes, core, 0, keepdims=False)
    given = lax.dynamic_index_in_dim(planes, 1 - core, 0, keepdims=False)
    partial = jnp.stack(by_core(local, core_swap(local)), axis=2).reshape(2, 4)
    chunk = jnp.concatenate(by_core(kept, core_swap(given)), axis=2).reshape(
        rows, 4 * own_chans, cols
    )
    before, after = edge_rows(chunk[:1], chunk[rows - 1 :], strip_at % 2 == 0)
    total = sum_over_strips(sum_over(partial, "frame"))
    in_count = frames * rows * cols * spread * per_group
    side = kernel_call(
        functools.partial(side_kernel, count_all=in_count),
        jax.ShapeDtypeStruct((3, 4 * own_chans, cols), jnp.bfloat16),
        (),
        jnp.broadcast_to(total[:, :, None], (2, 4, cols)),
        before,
        after,
        limit=4,
    )

    ahead, behind = (1, -1), (-1, 1)
    z_piece = z_swap(chunk)
    a_piece = from_x(chunk, ahead)
    b_piece = from_x(chunk, behind)
    az_piece = from_x(z_piece, ahead)
    bz_piece = from_x(z_piece, behind)
    d_piece = from_x(a_piece, ahead)
    dz_piece = from_x(bz_piece, behind)
    own_sides = kernel_call(
        pair_kernel,
        jax.ShapeDtypeStruct((2, 3, 4 * own_chans, cols), jnp.bfloat16),
        (),
        side,
        z_swap(side),
        limit=4,
    )
    a_sides = from_x(own_sides, ahead)
    b_sides = from_x(own_sides, behind)
    d_sides = from_x(own_sides, (2, 2))
    width = 2 * channels
    step_word = step_at.astype(jnp.int32)[None]
    core_word = core.astype(jnp.int32)[None]
    second_weight, near_weight = kernel_call(
        second_weights_kernel,
        (
            jax.ShapeDtypeStruct((3 * channels, 3 * channels), jnp.bfloat16),
            jax.ShapeDtypeStruct((2 * channels, 3 * channels), jnp.bfloat16),
        ),
        (2,),
        conv_second.reshape(3, 3 * channels, channels),
        temporal_weight,
        core_word,
        limit=6,
    )

    half_chans = channels // 2
    freq_table = jnp.exp(
        -math.log(10000.0) * jnp.arange(half_chans, dtype=jnp.float32) / half_chans
    )
    angle_rows = timesteps.astype(jnp.float32)[:, None] * freq_table[None, :]
    sinus_rows = jnp.concatenate([jnp.cos(angle_rows), jnp.sin(angle_rows)], axis=1).astype(
        jnp.bfloat16
    )
    wide_one = jnp.dot(sinus_rows, time_first, preferred_element_type=jnp.float32)
    embed_one = jax.nn.silu(wide_one).astype(jnp.bfloat16)
    embed_two = jax.nn.silu(
        jnp.dot(embed_one, time_second, preferred_element_type=jnp.float32)
    ).astype(jnp.bfloat16)
    embed = jnp.dot(embed_two, embed_proj, preferred_element_type=jnp.float32)[0]
    embeds = jnp.stack([embed, core_swap(embed)])
    embed_wide = jnp.broadcast_to(embeds[:, :, None], (2, channels, cols))

    bf16_rows = jax.ShapeDtypeStruct((rows, channels, cols), jnp.bfloat16)
    f32_rows = jax.ShapeDtypeStruct((rows, channels, cols), jnp.float32)
    act, plain = kernel_call(
        norm_kernel,
        (
            jax.ShapeDtypeStruct((rows + 2, width, cols), jnp.float32),
            jax.ShapeDtypeStruct((rows, width, cols), jnp.float32),
        ),
        (0, 1),
        step_word, keep, chunk, z_piece, a_piece, az_piece, b_piece, bz_piece, d_piece, dz_piece,
        own_sides, a_sides, b_sides, d_sides,
        work=4000000000,
        limit=4,
    )
    bf16_rows = jax.ShapeDtypeStruct((rows, channels, cols), jnp.bfloat16)
    conv_own, side_own, sums = kernel_call(
        first_kernel,
        (
            bf16_rows,
            bf16_rows,
            jax.ShapeDtypeStruct((2, 2, GROUPS, cols), jnp.float32),
        ),
        (),
        act, plain, embed_wide, conv_first.reshape(3, 3 * channels, width), skip_weight,
        scratch=(
            pltpu.VMEM(((rows + 1) * width, 256), jnp.bfloat16),
            pltpu.VMEM((rows // 2 * width, 256), jnp.bfloat16),
            pltpu.VMEM((4, channels, cols), jnp.float32),
            pltpu.VMEM((3 * channels, 3 * width), jnp.bfloat16),
            pltpu.SemaphoreType.DMA((3,)),
        ),
        work=4200000000,
        limit=14,
        hbm=(3,),
    )

    mine = sums[0] + core_swap(sums[1])
    mine = sum_over_strips(sum_over(mine, "frame"))
    mid_count = frames * rows * cols * spread * (channels // GROUPS)

    upper = jnp.broadcast_to(keep[3:].reshape(1, 1), (channels, cols)) > 0.5
    beside = link_swap(jnp.where(upper, conv_own[rows - 1], conv_own[0]))
    across = z_swap(beside)
    up = jnp.where(upper, across, beside)
    down = jnp.where(upper, beside, across)
    rims = jnp.stack([up, down])
    conv_other = core_swap(conv_own)
    side_other = core_swap(side_own)
    rims_other = core_swap(rims)

    conv_far = to_next_group(conv_own)
    rims_far = to_next_group(rims)

    def second_conv(conv, rims, outs):
        return kernel_call(
            functools.partial(second_kernel, count_all=mid_count),
            outs,
            (0,),
            keep, conv, rims[0], rims[1], mine, embed_wide, second_weight,
            scratch=(pltpu.VMEM(((rows + 1) * channels, 256), jnp.bfloat16),),
            work=2000000000,
            limit=6,
        )

    f32_rows = jax.ShapeDtypeStruct((rows, channels, cols), jnp.float32)
    second_own, temporal_own = second_conv(conv_own, rims, (f32_rows, bf16_rows))
    other_side = to_frames(temporal_own, (-1, 1))
    second_other, temporal_other = second_conv(conv_other, rims_other, (f32_rows, bf16_rows))
    (temporal_far,) = second_conv(conv_far, rims_far, (bf16_rows,))
    own_block, base = kernel_call(
        near_kernel,
        (jax.ShapeDtypeStruct((channels, rows, cols), jnp.bfloat16), f32_rows),
        (),
        temporal_own, temporal_other, temporal_far, second_own, second_other,
        side_own, side_other, near_weight,
        limit=8,
    )
    decoded = kernel_call(
        far_kernel,
        jax.ShapeDtypeStruct((channels, 2, rows, cols), jnp.bfloat16),
        (0,),
        core_word, other_side, base, own_block, temporal_weight,
        limit=8,
    )
    return decoded[None]


def solution(mesh):
    return jax.shard_map(
        on_device,
        mesh=mesh,
        in_specs=(
            P("step", "frame", "strip", None),
            P("step", "frame", "strip", None),
            P("step"),
            P(),
            P(),
            P(),
            P(),
            P(),
            P(),
            P(),
        ),
        out_specs=P("step", None, "frame", "strip", None),
        check_vma=False,
    )
```

```python
import functools
import math

import jax
import jax.numpy as jnp
from jax import lax
from jax.experimental import pallas as pl
from jax.experimental.pallas import tpu as pltpu
from jax.sharding import PartitionSpec as P


GROUPS = 32

norm_eps = 1e-05


IN_VMEM = pl.BlockSpec(memory_space=pltpu.VMEM)
IN_HBM = pl.BlockSpec(memory_space=pltpu.HBM)
IN_SMEM = pl.BlockSpec(memory_space=pltpu.SMEM)


def step_index(z, x, core):
    return z * 8 + x % 4 * 2 + core


def core_swap(values):
    return lax.ppermute(values, "step", [(i, i ^ 1) for i in range(16)])


def z_swap(values):
    return lax.ppermute(values, "step", [(i, i ^ 8) for i in range(16)])


def from_x(values, shifts):
    pairs = [
        (step_index(z, x + shifts[core], core), step_index(z, x, core))
        for z in range(2)
        for x in range(4)
        for core in range(2)
    ]
    return lax.ppermute(values, "step", pairs)


def to_frames(values, shifts):
    count = lax.axis_size("frame")
    pairs = []
    for step in range(16):
        for frame in range(count):
            target = frame + shifts[step % 2]
            if 0 <= target < count:
                pairs.append((step * count + frame, step * count + target))
    return lax.ppermute(values, ("step", "frame"), pairs)


def to_next_group(values):
    count = lax.axis_size("frame")
    pairs = []
    for step in range(16):
        for frame in range(count):
            target = frame + (-1, 1)[step % 2]
            if 0 <= target < count:
                pairs.append((step * count + frame, (step ^ 1) * count + target))
    return lax.ppermute(values, ("step", "frame"), pairs)


def sum_over(values, axis):
    count = lax.axis_size(axis)
    total = values
    for k in range(1, count):
        total = total + lax.ppermute(values, axis, [(i, (i + k) % count) for i in range(count)])
    return total


def link_swap(values):
    count = lax.axis_size("strip")
    pairs = []
    for step in range(16):
        for strip in range(count):
            beside = (strip + 1 if step >= 8 else strip - 1) % count
            pairs.append((step * count + strip, (step ^ 8) * count + beside))
    return lax.ppermute(values, ("step", "strip"), pairs)


def sum_over_strips(values):
    values = values + lax.ppermute(values, "strip", [(0, 1), (1, 0), (2, 3), (3, 2)])
    return values + lax.ppermute(values, "strip", [(1, 2), (2, 1), (3, 0), (0, 3)])


def edge_rows(first, last, even):
    one = lax.ppermute(jnp.where(even, last, first), "strip", [(0, 1), (1, 0), (2, 3), (3, 2)])
    two = lax.ppermute(jnp.where(even, first, last), "strip", [(1, 2), (2, 1), (3, 0), (0, 3)])
    return jnp.where(even, two, one), jnp.where(even, one, two)


def silu(v):
    return v * (0.5 * jnp.tanh(0.5 * v) + 0.5)


def join_columns(acc, half, outs):
    lanes = slice(half * 128, half * 128 + 128)
    lane = lax.broadcasted_iota(jnp.int32, (outs, 128), 1)
    left = pltpu.roll(acc[0:outs, lanes], 1, axis=1)
    right = pltpu.roll(acc[2 * outs : 3 * outs, lanes], 127, axis=1)
    return (
        acc[outs : 2 * outs, lanes]
        + jnp.where(lane == 0, 0.0, left)
        + jnp.where(lane == 127, 0.0, right)
    )


def one_hot(rows, cols, per, by_row):
    row = lax.broadcasted_iota(jnp.int32, (rows, cols), 0)
    col = lax.broadcasted_iota(jnp.int32, (rows, cols), 1)
    low, high = (col * per, row) if by_row else (row * per, col)
    return ((high >= low) & (high < low + per)).astype(jnp.float32)


def exact_dot(a, b):
    return jnp.dot(a, b, precision=lax.Precision.HIGHEST, preferred_element_type=jnp.float32)


def side_kernel(totals_ref, before_ref, after_ref, out_ref, *, count_all):
    chans = out_ref.shape[1]
    out_ref[0] = before_ref[0]
    out_ref[1] = after_ref[0]
    mean = totals_ref[0] / count_all
    scale = lax.rsqrt(totals_ref[1] / count_all - mean * mean + norm_eps)
    chan = lax.broadcasted_iota(jnp.int32, (chans, 128), 0)
    lane = lax.broadcasted_iota(jnp.int32, (chans, 128), 1)
    per = chans // 4
    plane = jnp.zeros((chans, 128), jnp.float32)
    for which, values in enumerate((mean, scale)):
        wide = jnp.zeros((chans, 128), jnp.float32)
        for group in range(4):
            inside = (chan >= group * per) & (chan < (group + 1) * per)
            wide = jnp.where(inside, values[group : group + 1, :], wide)
        for part in range(3):
            piece = wide.astype(jnp.bfloat16).astype(jnp.float32)
            plane = jnp.where(lane == which * 3 + part, piece, plane)
            wide = wide - piece
    out_ref[2] = plane.astype(jnp.bfloat16)


def second_weights_kernel(second_ref, temporal_ref, core_ref, out_ref, near_ref):
    width = second_ref.shape[2]
    out_ref[...] = jnp.concatenate([second_ref[0], second_ref[1], second_ref[2]], axis=1)
    side = 2 - 2 * core_ref[0]
    middle = temporal_ref[1]
    here, there = temporal_ref[side], temporal_ref[2 - side]
    near_ref[0:width, :] = jnp.concatenate([middle, here, there], axis=1)
    near_ref[width : 2 * width, :] = jnp.concatenate([there, middle, there * 0], axis=1)


def pair_kernel(one_ref, two_ref, out_ref):
    out_ref[0] = one_ref[...]
    out_ref[1] = two_ref[...]


def norm_kernel(step_ref, keep_ref, *refs):
    pieces, sides, (act_ref, plain_ref) = refs[:8], refs[8:12], refs[12:]
    chans = act_ref.shape[1]
    rows = plain_ref.shape[0]
    per = pieces[0].shape[1] // 2
    lane = lax.broadcasted_iota(jnp.int32, (per, 128), 1)
    step = step_ref[0]
    z_at, x_at = step >> 3, step >> 1
    turn = 1 - 2 * (step & 1)
    for slot, ref in enumerate(pieces):
        x_from = (x_at + (0, turn, 4 - turn, 2)[slot // 2]) & 3
        place = (z_at ^ (slot % 2)) * 4 + x_from
        side_ref = sides[slot // 2]
        for kind in range(2):
            here = slice(kind * per, (kind + 1) * per)
            at = pl.multiple_of(place * per, 8) + kind * (chans // 2)
            at = pl.multiple_of(at, 8)
            part = side_ref[slot % 2, 2, here, :].astype(jnp.float32)
            mean = jnp.sum(jnp.where(lane < 3, part, 0.0), axis=1, keepdims=True)
            rstd = jnp.sum(jnp.where((lane >= 3) & (lane < 6), part, 0.0), axis=1, keepdims=True)
            for edge, row in enumerate((0, rows + 1)):
                raw = side_ref[slot % 2, edge, here, :].astype(jnp.float32)
                act_ref[row, pl.ds(at, per), :] = silu((raw - mean) * rstd) * keep_ref[edge]

            def inner(row, carry, ref=ref, here=here, at=at, mean=mean, rstd=rstd):
                raw = ref[row, here, :].astype(jnp.float32)
                act_ref[row + 1, pl.ds(at, per), :] = silu((raw - mean) * rstd)
                plain_ref[row, pl.ds(at, per), :] = raw
                return carry

            lax.fori_loop(0, rows, inner, 0, unroll=True)


def first_kernel(
    act_ref, plain_ref, embed_ref, first_ref, skip_weight_ref,
    conv_ref, skip_ref, sums_ref,
    wide_ref, raw_ref, total_ref, weight_ref, sem,
):
    chans = act_ref.shape[1]
    rows = conv_ref.shape[0]
    outs = conv_ref.shape[1]
    copies = [
        pltpu.make_async_copy(
            first_ref.at[tap], weight_ref.at[:, tap * chans : (tap + 1) * chans], sem.at[tap]
        )
        for tap in range(3)
    ]
    for copy in copies:
        copy.start()
    for row in range(rows + 2):
        act = act_ref[row].astype(jnp.bfloat16)
        if row < rows + 1:
            wide_ref[row * chans : (row + 1) * chans, 0:128] = act
        if row > 0:
            wide_ref[(row - 1) * chans : row * chans, 128:256] = act
    for row in range(rows):
        lanes = slice(row % 2 * 128, row % 2 * 128 + 128)
        pair = row // 2
        raw_ref[pair * chans : (pair + 1) * chans, lanes] = plain_ref[row].astype(jnp.bfloat16)
    total_ref[...] = jnp.zeros_like(total_ref)
    for copy in copies:
        copy.wait()
    for pair in range(rows // 2):
        acc = jnp.dot(
            weight_ref[...],
            wide_ref[2 * pair * chans : (2 * pair + 3) * chans, :],
            preferred_element_type=jnp.float32,
        )
        skip = jnp.dot(
            skip_weight_ref[...],
            raw_ref[pair * chans : (pair + 1) * chans, :],
            preferred_element_type=jnp.float32,
        ).astype(jnp.bfloat16)
        for half in range(2):
            row = 2 * pair + half
            out = join_columns(acc, half, outs)
            conv_ref[row] = out.astype(jnp.bfloat16)
            skip_ref[row] = skip[:, half * 128 : half * 128 + 128]
            for who in range(2):
                hidden = out + embed_ref[who]
                total_ref[2 * who] += hidden
                total_ref[2 * who + 1] += hidden * hidden
    gather = one_hot(GROUPS, outs, outs // GROUPS, False)
    for which in range(4):
        sums_ref[which // 2, which % 2] = exact_dot(gather, total_ref[which])


def second_kernel(
    keep_ref, conv_ref, before_ref, after_ref, sums_ref, embed_ref, weight_ref,
    *outs, count_all,
):
    wide_ref, temporal_ref = outs[-1], outs[-2]
    far = len(outs) == 2
    rows, chans = conv_ref.shape[0], conv_ref.shape[1]
    mean = jnp.sum(sums_ref[0], axis=1, keepdims=True) / count_all
    square = jnp.sum(sums_ref[1], axis=1, keepdims=True) / count_all
    scale = lax.rsqrt(square - mean * mean + norm_eps)
    spread = one_hot(chans, GROUPS, chans // GROUPS, True)
    lanes = (GROUPS, 128)
    shift = embed_ref[0] - exact_dot(spread, jnp.broadcast_to(mean, lanes))
    rstd = exact_dot(spread, jnp.broadcast_to(scale, lanes))
    for row in range(rows + 2):
        if row == 0:
            raw = before_ref[...]
        elif row == rows + 1:
            raw = after_ref[...]
        else:
            raw = conv_ref[row - 1]
        act = silu((raw.astype(jnp.float32) + shift) * rstd)
        if row == 0:
            act = act * keep_ref[0]
        if row == rows + 1:
            act = act * keep_ref[1]
        act = act.astype(jnp.bfloat16)
        if row < rows + 1:
            wide_ref[row * chans : (row + 1) * chans, 0:128] = act
        if row > 0:
            wide_ref[(row - 1) * chans : row * chans, 128:256] = act

    def one_pair(pair, carry):
        at = pl.multiple_of(2 * pair * chans, 16)
        acc = jnp.dot(
            weight_ref[...],
            wide_ref[pl.ds(at, 3 * chans), :],
            preferred_element_type=jnp.float32,
        )
        for half in range(2):
            row = 2 * pair + half
            out = join_columns(acc, half, chans)
            if far:
                temporal_ref[row] = (silu(out) * keep_ref[2]).astype(jnp.bfloat16)
            else:
                outs[0][row] = out
                temporal_ref[row] = silu(out).astype(jnp.bfloat16)
        return carry

    lax.fori_loop(0, rows // 2, one_pair, 0, unroll=2)


def turned(lines):
    return jnp.transpose(jnp.stack(lines), (1, 0, 2)).astype(jnp.bfloat16)


def near_kernel(
    t0_ref, t1_ref, t2_ref, s0_ref, s1_ref, k0_ref, k1_ref, weight_ref, own_ref, base_ref
):
    rows, chans = t0_ref.shape[0], t0_ref.shape[1]
    lines = []
    for pair in range(rows // 2):
        a, b = 2 * pair, 2 * pair + 1
        sides = jnp.concatenate(
            [jnp.concatenate([ref[a], ref[b]], axis=1) for ref in (t0_ref, t1_ref, t2_ref)], axis=0
        )
        acc = jnp.dot(weight_ref[...], sides, preferred_element_type=jnp.float32)
        for half in range(2):
            row = 2 * pair + half
            lanes = slice(half * 128, half * 128 + 128)
            lines.append(acc[0:chans, lanes] + s0_ref[row] + k0_ref[row].astype(jnp.float32))
            base_ref[row] = acc[chans:, lanes] + s1_ref[row] + k1_ref[row].astype(jnp.float32)
    own_ref[...] = turned(lines)


def far_kernel(core_ref, side_ref, base_ref, own_ref, weight_ref, out_ref):
    rows = side_ref.shape[0]
    core = core_ref[0]
    weight = weight_ref[2 - 2 * core]
    out_ref[:, pl.ds(core, 1), :, :] = own_ref[...][:, None]
    lines = []
    for pair in range(rows // 2):
        side = jnp.concatenate([side_ref[2 * pair], side_ref[2 * pair + 1]], axis=1)
        acc = jnp.dot(weight, side, preferred_element_type=jnp.float32)
        for half in range(2):
            lanes = slice(half * 128, half * 128 + 128)
            lines.append(acc[:, lanes] + base_ref[2 * pair + half])
    out_ref[:, pl.ds(1 - core, 1), :, :] = turned(lines)[:, None]


def kernel_call(body, outs, smem, *args, scratch=(), limit=16, hbm=(), work=0):
    specs = [IN_SMEM if i in smem else IN_HBM if i in hbm else IN_VMEM for i in range(len(args))]
    return pl.pallas_call(
        body,
        out_shape=outs,
        in_specs=specs,
        out_specs=jax.tree.map(lambda _: IN_VMEM, outs),
        scratch_shapes=list(scratch),
        cost_estimate=pl.CostEstimate(
            flops=work or 1000000,
            transcendentals=0,
            bytes_accessed=sum(math.prod(a.shape) * a.dtype.itemsize for a in args),
        ),
        compiler_params=pltpu.CompilerParams(vmem_limit_bytes=limit << 20),
    )(*args)


def on_device(
    enc_feats, skip_feats, timesteps, time_first, time_second, embed_proj,
    conv_first, conv_second, temporal_weight, skip_weight,
):
    channels = conv_second.shape[2]
    own_chans, frames, rows, cols = enc_feats.shape
    spread = lax.axis_size("frame") * lax.axis_size("strip")
    step_at = lax.axis_index("step")
    core, z_at = step_at % 2, step_at // 8
    strip_at = lax.axis_index("strip")
    frame_at = lax.axis_index("frame")
    keep = jnp.stack(
        [
            strip_at > 0,
            strip_at < lax.axis_size("strip") - 1,
            jnp.where(core == 0, frame_at > 0, frame_at < lax.axis_size("frame") - 1),
            z_at == 1,
        ]
    ).astype(jnp.float32)
    per_group = 2 * channels // GROUPS

    joined = jnp.stack([enc_feats, skip_feats])
    wide = joined.astype(jnp.float32)
    local = jnp.stack([jnp.sum(wide, axis=(1, 2, 3, 4)), jnp.sum(wide * wide, axis=(1, 2, 3, 4))])

    def by_core(mine, theirs):
        return jnp.where(core == 0, mine, theirs), jnp.where(core == 0, theirs, mine)

    planes = jnp.transpose(joined, (2, 3, 0, 1, 4))
    kept = lax.dynamic_index_in_dim(planes, core, 0, keepdims=False)
    given = lax.dynamic_index_in_dim(planes, 1 - core, 0, keepdims=False)
    partial = jnp.stack(by_core(local, core_swap(local)), axis=2).reshape(2, 4)
    taken = core_swap(given)
    chunk = jnp.concatenate(by_core(kept, taken), axis=2)
    chunk = chunk.reshape(rows, 4 * own_chans, cols)
    before, after = edge_rows(chunk[:1], chunk[rows - 1 :], strip_at % 2 == 0)
    total = sum_over_strips(sum_over(partial, "frame"))
    in_count = frames * rows * cols * spread * per_group
    side = kernel_call(
        functools.partial(side_kernel, count_all=in_count),
        jax.ShapeDtypeStruct((3, 4 * own_chans, cols), jnp.bfloat16),
        (),
        jnp.broadcast_to(total[:, :, None], (2, 4, cols)),
        before,
        after,
        limit=4,
    )

    ahead, behind = (1, -1), (-1, 1)
    z_piece = z_swap(chunk)
    a_piece = from_x(chunk, ahead)
    b_piece = from_x(chunk, behind)
    az_piece = from_x(z_piece, ahead)
    bz_piece = from_x(z_piece, behind)
    d_piece = from_x(a_piece, ahead)
    dz_piece = from_x(bz_piece, behind)
    own_sides = kernel_call(
        pair_kernel,
        jax.ShapeDtypeStruct((2, 3, 4 * own_chans, cols), jnp.bfloat16),
        (),
        side,
        z_swap(side),
        limit=4,
    )
    a_sides = from_x(own_sides, ahead)
    b_sides = from_x(own_sides, behind)
    d_sides = from_x(own_sides, (2, 2))
    width = 2 * channels
    step_word = step_at.astype(jnp.int32)[None]
    core_word = core.astype(jnp.int32)[None]
    second_weight, near_weight = kernel_call(
        second_weights_kernel,
        (
            jax.ShapeDtypeStruct((3 * channels, 3 * channels), jnp.bfloat16),
            jax.ShapeDtypeStruct((2 * channels, 3 * channels), jnp.bfloat16),
        ),
        (2,),
        conv_second.reshape(3, 3 * channels, channels),
        temporal_weight,
        core_word,
        limit=6,
    )

    half_chans = channels // 2
    freq_table = jnp.exp(
        -math.log(10000.0) * jnp.arange(half_chans, dtype=jnp.float32) / half_chans
    )
    angle_rows = timesteps.astype(jnp.float32)[:, None] * freq_table[None, :]
    sinus_rows = jnp.concatenate([jnp.cos(angle_rows), jnp.sin(angle_rows)], axis=1).astype(
        jnp.bfloat16
    )
    wide_one = jnp.dot(sinus_rows, time_first, preferred_element_type=jnp.float32)
    embed_one = jax.nn.silu(wide_one).astype(jnp.bfloat16)
    embed_two = jax.nn.silu(
        jnp.dot(embed_one, time_second, preferred_element_type=jnp.float32)
    ).astype(jnp.bfloat16)
    embed = jnp.dot(embed_two, embed_proj, preferred_element_type=jnp.float32)[0]
    embeds = jnp.stack([embed, core_swap(embed)])
    embed_wide = jnp.broadcast_to(embeds[:, :, None], (2, channels, cols))

    bf16_rows = jax.ShapeDtypeStruct((rows, channels, cols), jnp.bfloat16)
    f32_rows = jax.ShapeDtypeStruct((rows, channels, cols), jnp.float32)
    act, plain = kernel_call(
        norm_kernel,
        (
            jax.ShapeDtypeStruct((rows + 2, width, cols), jnp.float32),
            jax.ShapeDtypeStruct((rows, width, cols), jnp.float32),
        ),
        (0, 1),
        step_word, keep, chunk, z_piece, a_piece, az_piece, b_piece, bz_piece, d_piece, dz_piece,
        own_sides, a_sides, b_sides, d_sides,
        work=4000000000,
        limit=4,
    )
    bf16_rows = jax.ShapeDtypeStruct((rows, channels, cols), jnp.bfloat16)
    conv_own, side_own, sums = kernel_call(
        first_kernel,
        (
            bf16_rows,
            bf16_rows,
            jax.ShapeDtypeStruct((2, 2, GROUPS, cols), jnp.float32),
        ),
        (),
        act, plain, embed_wide, conv_first.reshape(3, 3 * channels, width), skip_weight,
        scratch=(
            pltpu.VMEM(((rows + 1) * width, 256), jnp.bfloat16),
            pltpu.VMEM((rows // 2 * width, 256), jnp.bfloat16),
            pltpu.VMEM((4, channels, cols), jnp.float32),
            pltpu.VMEM((3 * channels, 3 * width), jnp.bfloat16),
            pltpu.SemaphoreType.DMA((3,)),
        ),
        work=4200000000,
        limit=14,
        hbm=(3,),
    )

    mine = sums[0] + core_swap(sums[1])
    mine = sum_over_strips(sum_over(mine, "frame"))
    mid_count = frames * rows * cols * spread * (channels // GROUPS)

    upper = jnp.broadcast_to(keep[3:].reshape(1, 1), (channels, cols)) > 0.5
    beside = link_swap(jnp.where(upper, conv_own[rows - 1], conv_own[0]))
    across = z_swap(beside)
    up = jnp.where(upper, across, beside)
    down = jnp.where(upper, beside, across)
    rims = jnp.stack([up, down])
    conv_other = core_swap(conv_own)
    side_other = core_swap(side_own)
    rims_other = core_swap(rims)

    conv_far = to_next_group(conv_own)
    rims_far = to_next_group(rims)

    def second_conv(conv, rims, outs):
        return kernel_call(
            functools.partial(second_kernel, count_all=mid_count),
            outs,
            (0,),
            keep, conv, rims[0], rims[1], mine, embed_wide, second_weight,
            scratch=(pltpu.VMEM(((rows + 1) * channels, 256), jnp.bfloat16),),
            work=2000000000,
            limit=6,
        )

    f32_rows = jax.ShapeDtypeStruct((rows, channels, cols), jnp.float32)
    second_own, temporal_own = second_conv(conv_own, rims, (f32_rows, bf16_rows))
    other_side = to_frames(temporal_own, (-1, 1))
    second_other, temporal_other = second_conv(conv_other, rims_other, (f32_rows, bf16_rows))
    (temporal_far,) = second_conv(conv_far, rims_far, (bf16_rows,))
    own_block, base = kernel_call(
        near_kernel,
        (jax.ShapeDtypeStruct((channels, rows, cols), jnp.bfloat16), f32_rows),
        (),
        temporal_own, temporal_other, temporal_far, second_own, second_other,
        side_own, side_other, near_weight,
        limit=8,
    )
    decoded = kernel_call(
        far_kernel,
        jax.ShapeDtypeStruct((channels, 2, rows, cols), jnp.bfloat16),
        (0,),
        core_word, other_side, base, own_block, temporal_weight,
        limit=8,
    )
    return decoded[None]


def solution(mesh):
    return jax.shard_map(
        on_device,
        mesh=mesh,
        in_specs=(
            P("step", "frame", "strip", None),
            P("step", "frame", "strip", None),
            P("step"),
            P(),
            P(),
            P(),
            P(),
            P(),
            P(),
            P(),
        ),
        out_specs=P("step", None, "frame", "strip", None),
        check_vma=False,
    )
```

```python
import functools
import math

import jax
import jax.numpy as jnp
from jax import lax
from jax.experimental import pallas as pl
from jax.experimental.pallas import tpu as pltpu
from jax.sharding import PartitionSpec as P


GROUPS = 32

norm_eps = 1e-05


IN_VMEM = pl.BlockSpec(memory_space=pltpu.VMEM)
IN_HBM = pl.BlockSpec(memory_space=pltpu.HBM)
IN_SMEM = pl.BlockSpec(memory_space=pltpu.SMEM)


def step_index(z, x, core):
    return z * 8 + x % 4 * 2 + core


def core_swap(values):
    return lax.ppermute(values, "step", [(i, i ^ 1) for i in range(16)])


def z_swap(values):
    return lax.ppermute(values, "step", [(i, i ^ 8) for i in range(16)])


def from_x(values, shifts):
    pairs = [
        (step_index(z, x + shifts[core], core), step_index(z, x, core))
        for z in range(2)
        for x in range(4)
        for core in range(2)
    ]
    return lax.ppermute(values, "step", pairs)


def to_frames(values, shifts):
    count = lax.axis_size("frame")
    pairs = []
    for step in range(16):
        for frame in range(count):
            target = frame + shifts[step % 2]
            if 0 <= target < count:
                pairs.append((step * count + frame, step * count + target))
    return lax.ppermute(values, ("step", "frame"), pairs)


def to_next_group(values):
    count = lax.axis_size("frame")
    pairs = []
    for step in range(16):
        for frame in range(count):
            target = frame + (-1, 1)[step % 2]
            if 0 <= target < count:
                pairs.append((step * count + frame, (step ^ 1) * count + target))
    return lax.ppermute(values, ("step", "frame"), pairs)


def sum_over(values, axis):
    count = lax.axis_size(axis)
    total = values
    for k in range(1, count):
        total = total + lax.ppermute(values, axis, [(i, (i + k) % count) for i in range(count)])
    return total


def link_swap(values):
    count = lax.axis_size("strip")
    pairs = []
    for step in range(16):
        for strip in range(count):
            beside = (strip + 1 if step >= 8 else strip - 1) % count
            pairs.append((step * count + strip, (step ^ 8) * count + beside))
    return lax.ppermute(values, ("step", "strip"), pairs)


def sum_over_strips(values):
    values = values + lax.ppermute(values, "strip", [(0, 1), (1, 0), (2, 3), (3, 2)])
    return values + lax.ppermute(values, "strip", [(1, 2), (2, 1), (3, 0), (0, 3)])


def edge_rows(first, last, even):
    one = lax.ppermute(jnp.where(even, last, first), "strip", [(0, 1), (1, 0), (2, 3), (3, 2)])
    two = lax.ppermute(jnp.where(even, first, last), "strip", [(1, 2), (2, 1), (3, 0), (0, 3)])
    return jnp.where(even, two, one), jnp.where(even, one, two)


def silu(v):
    return v * (0.5 * jnp.tanh(0.5 * v) + 0.5)


def join_columns(acc, half, outs):
    lanes = slice(half * 128, half * 128 + 128)
    lane = lax.broadcasted_iota(jnp.int32, (outs, 128), 1)
    left = pltpu.roll(acc[0:outs, lanes], 1, axis=1)
    right = pltpu.roll(acc[2 * outs : 3 * outs, lanes], 127, axis=1)
    return (
        acc[outs : 2 * outs, lanes]
        + jnp.where(lane == 0, 0.0, left)
        + jnp.where(lane == 127, 0.0, right)
    )


def one_hot(rows, cols, per, by_row):
    row = lax.broadcasted_iota(jnp.int32, (rows, cols), 0)
    col = lax.broadcasted_iota(jnp.int32, (rows, cols), 1)
    low, high = (col * per, row) if by_row else (row * per, col)
    return ((high >= low) & (high < low + per)).astype(jnp.float32)


def exact_dot(a, b):
    return jnp.dot(a, b, precision=lax.Precision.HIGHEST, preferred_element_type=jnp.float32)


def side_kernel(totals_ref, before_ref, after_ref, out_ref, *, count_all):
    chans = out_ref.shape[1]
    out_ref[0] = before_ref[0]
    out_ref[1] = after_ref[0]
    mean = totals_ref[0] / count_all
    scale = lax.rsqrt(totals_ref[1] / count_all - mean * mean + norm_eps)
    chan = lax.broadcasted_iota(jnp.int32, (chans, 128), 0)
    lane = lax.broadcasted_iota(jnp.int32, (chans, 128), 1)
    per = chans // 4
    plane = jnp.zeros((chans, 128), jnp.float32)
    for which, values in enumerate((mean, scale)):
        wide = jnp.zeros((chans, 128), jnp.float32)
        for group in range(4):
            inside = (chan >= group * per) & (chan < (group + 1) * per)
            wide = jnp.where(inside, values[group : group + 1, :], wide)
        for part in range(3):
            piece = wide.astype(jnp.bfloat16).astype(jnp.float32)
            plane = jnp.where(lane == which * 3 + part, piece, plane)
            wide = wide - piece
    out_ref[2] = plane.astype(jnp.bfloat16)


def second_weights_kernel(second_ref, temporal_ref, core_ref, out_ref, near_ref):
    width = second_ref.shape[2]
    out_ref[...] = jnp.concatenate([second_ref[0], second_ref[1], second_ref[2]], axis=1)
    side = 2 - 2 * core_ref[0]
    middle = temporal_ref[1]
    here, there = temporal_ref[side], temporal_ref[2 - side]
    near_ref[0:width, :] = jnp.concatenate([middle, here, there], axis=1)
    near_ref[width : 2 * width, :] = jnp.concatenate([there, middle, there * 0], axis=1)


def pair_kernel(one_ref, two_ref, out_ref):
    out_ref[0] = one_ref[...]
    out_ref[1] = two_ref[...]


def norm_kernel(step_ref, keep_ref, *refs):
    pieces, sides, (act_ref, plain_ref) = refs[:8], refs[8:12], refs[12:]
    chans = act_ref.shape[1]
    rows = plain_ref.shape[0]
    per = pieces[0].shape[1] // 2
    lane = lax.broadcasted_iota(jnp.int32, (per, 128), 1)
    step = step_ref[0]
    z_at, x_at = step >> 3, step >> 1
    turn = 1 - 2 * (step & 1)
    for slot, ref in enumerate(pieces):
        x_from = (x_at + (0, turn, 4 - turn, 2)[slot // 2]) & 3
        place = (z_at ^ (slot % 2)) * 4 + x_from
        side_ref = sides[slot // 2]
        for kind in range(2):
            here = slice(kind * per, (kind + 1) * per)
            at = pl.multiple_of(place * per, 8) + kind * (chans // 2)
            at = pl.multiple_of(at, 8)
            part = side_ref[slot % 2, 2, here, :].astype(jnp.float32)
            mean = jnp.sum(jnp.where(lane < 3, part, 0.0), axis=1, keepdims=True)
            rstd = jnp.sum(jnp.where((lane >= 3) & (lane < 6), part, 0.0), axis=1, keepdims=True)
            for edge, row in enumerate((0, rows + 1)):
                raw = side_ref[slot % 2, edge, here, :].astype(jnp.float32)
                act_ref[row, pl.ds(at, per), :] = silu((raw - mean) * rstd) * keep_ref[edge]

            def inner(row, carry, ref=ref, here=here, at=at, mean=mean, rstd=rstd):
                raw = ref[row, here, :].astype(jnp.float32)
                act_ref[row + 1, pl.ds(at, per), :] = silu((raw - mean) * rstd)
                plain_ref[row, pl.ds(at, per), :] = raw
                return carry

            lax.fori_loop(0, rows, inner, 0, unroll=True)


def first_kernel(
    act_ref, plain_ref, embed_ref, first_ref, skip_weight_ref,
    conv_ref, skip_ref, sums_ref,
    wide_ref, raw_ref, total_ref, weight_ref, sem,
):
    chans = act_ref.shape[1]
    rows = conv_ref.shape[0]
    outs = conv_ref.shape[1]
    copies = [
        pltpu.make_async_copy(
            first_ref.at[tap], weight_ref.at[:, tap * chans : (tap + 1) * chans], sem.at[tap]
        )
        for tap in range(3)
    ]
    for copy in copies:
        copy.start()
    for row in range(rows + 2):
        act = act_ref[row].astype(jnp.bfloat16)
        if row < rows + 1:
            wide_ref[row * chans : (row + 1) * chans, 0:128] = act
        if row > 0:
            wide_ref[(row - 1) * chans : row * chans, 128:256] = act
    for row in range(rows):
        lanes = slice(row % 2 * 128, row % 2 * 128 + 128)
        pair = row // 2
        raw_ref[pair * chans : (pair + 1) * chans, lanes] = plain_ref[row].astype(jnp.bfloat16)
    total_ref[...] = jnp.zeros_like(total_ref)
    for copy in copies:
        copy.wait()

    def one_pair(pair, carry):
        at = pl.multiple_of(2 * pair * chans, 16)
        acc = jnp.dot(
            weight_ref[...],
            wide_ref[pl.ds(at, 3 * chans), :],
            preferred_element_type=jnp.float32,
        )
        skip = jnp.dot(
            skip_weight_ref[...],
            raw_ref[pl.ds(pl.multiple_of(pair * chans, 16), chans), :],
            preferred_element_type=jnp.float32,
        ).astype(jnp.bfloat16)
        for half in range(2):
            row = 2 * pair + half
            out = join_columns(acc, half, outs)
            conv_ref[row] = out.astype(jnp.bfloat16)
            skip_ref[row] = skip[:, half * 128 : half * 128 + 128]
            for who in range(2):
                hidden = out + embed_ref[who]
                total_ref[2 * who] += hidden
                total_ref[2 * who + 1] += hidden * hidden
        return carry

    lax.fori_loop(0, rows // 2, one_pair, 0, unroll=2)
    gather = one_hot(GROUPS, outs, outs // GROUPS, False)
    for which in range(4):
        sums_ref[which // 2, which % 2] = exact_dot(gather, total_ref[which])


def second_kernel(
    keep_ref, conv_ref, before_ref, after_ref, sums_ref, embed_ref, weight_ref,
    *outs, count_all,
):
    wide_ref, temporal_ref = outs[-1], outs[-2]
    far = len(outs) == 2
    rows, chans = conv_ref.shape[0], conv_ref.shape[1]
    mean = jnp.sum(sums_ref[0], axis=1, keepdims=True) / count_all
    square = jnp.sum(sums_ref[1], axis=1, keepdims=True) / count_all
    scale = lax.rsqrt(square - mean * mean + norm_eps)
    spread = one_hot(chans, GROUPS, chans // GROUPS, True)
    lanes = (GROUPS, 128)
    shift = embed_ref[0] - exact_dot(spread, jnp.broadcast_to(mean, lanes))
    rstd = exact_dot(spread, jnp.broadcast_to(scale, lanes))
    for row in range(rows + 2):
        if row == 0:
            raw = before_ref[...]
        elif row == rows + 1:
            raw = after_ref[...]
        else:
            raw = conv_ref[row - 1]
        act = silu((raw.astype(jnp.float32) + shift) * rstd)
        if row == 0:
            act = act * keep_ref[0]
        if row == rows + 1:
            act = act * keep_ref[1]
        act = act.astype(jnp.bfloat16)
        if row < rows + 1:
            wide_ref[row * chans : (row + 1) * chans, 0:128] = act
        if row > 0:
            wide_ref[(row - 1) * chans : row * chans, 128:256] = act

    def one_pair(pair, carry):
        at = pl.multiple_of(2 * pair * chans, 16)
        acc = jnp.dot(
            weight_ref[...],
            wide_ref[pl.ds(at, 3 * chans), :],
            preferred_element_type=jnp.float32,
        )
        for half in range(2):
            row = 2 * pair + half
            out = join_columns(acc, half, chans)
            if far:
                temporal_ref[row] = (silu(out) * keep_ref[2]).astype(jnp.bfloat16)
            else:
                outs[0][row] = out
                temporal_ref[row] = silu(out).astype(jnp.bfloat16)
        return carry

    lax.fori_loop(0, rows // 2, one_pair, 0, unroll=True)


def turned(lines):
    return jnp.transpose(jnp.stack(lines), (1, 0, 2)).astype(jnp.bfloat16)


def near_kernel(
    t0_ref, t1_ref, t2_ref, s0_ref, s1_ref, k0_ref, k1_ref, weight_ref, own_ref, base_ref
):
    rows, chans = t0_ref.shape[0], t0_ref.shape[1]
    lines = []
    for pair in range(rows // 2):
        a, b = 2 * pair, 2 * pair + 1
        sides = jnp.concatenate(
            [jnp.concatenate([ref[a], ref[b]], axis=1) for ref in (t0_ref, t1_ref, t2_ref)], axis=0
        )
        acc = jnp.dot(weight_ref[...], sides, preferred_element_type=jnp.float32)
        for half in range(2):
            row = 2 * pair + half
            lanes = slice(half * 128, half * 128 + 128)
            lines.append(acc[0:chans, lanes] + s0_ref[row] + k0_ref[row].astype(jnp.float32))
            base_ref[row] = acc[chans:, lanes] + s1_ref[row] + k1_ref[row].astype(jnp.float32)
    own_ref[...] = turned(lines)


def far_kernel(core_ref, side_ref, base_ref, own_ref, weight_ref, out_ref):
    rows = side_ref.shape[0]
    core = core_ref[0]
    weight = weight_ref[2 - 2 * core]
    out_ref[:, pl.ds(core, 1), :, :] = own_ref[...][:, None]
    lines = []
    for pair in range(rows // 2):
        side = jnp.concatenate([side_ref[2 * pair], side_ref[2 * pair + 1]], axis=1)
        acc = jnp.dot(weight, side, preferred_element_type=jnp.float32)
        for half in range(2):
            lanes = slice(half * 128, half * 128 + 128)
            lines.append(acc[:, lanes] + base_ref[2 * pair + half])
    out_ref[:, pl.ds(1 - core, 1), :, :] = turned(lines)[:, None]


def kernel_call(body, outs, smem, *args, scratch=(), limit=16, hbm=(), work=0):
    specs = [IN_SMEM if i in smem else IN_HBM if i in hbm else IN_VMEM for i in range(len(args))]
    return pl.pallas_call(
        body,
        out_shape=outs,
        in_specs=specs,
        out_specs=jax.tree.map(lambda _: IN_VMEM, outs),
        scratch_shapes=list(scratch),
        cost_estimate=pl.CostEstimate(
            flops=work or 1000000,
            transcendentals=0,
            bytes_accessed=sum(math.prod(a.shape) * a.dtype.itemsize for a in args),
        ),
        compiler_params=pltpu.CompilerParams(vmem_limit_bytes=limit << 20),
    )(*args)


def on_device(
    enc_feats, skip_feats, timesteps, time_first, time_second, embed_proj,
    conv_first, conv_second, temporal_weight, skip_weight,
):
    channels = conv_second.shape[2]
    own_chans, frames, rows, cols = enc_feats.shape
    spread = lax.axis_size("frame") * lax.axis_size("strip")
    step_at = lax.axis_index("step")
    core, z_at = step_at % 2, step_at // 8
    strip_at = lax.axis_index("strip")
    frame_at = lax.axis_index("frame")
    keep = jnp.stack(
        [
            strip_at > 0,
            strip_at < lax.axis_size("strip") - 1,
            jnp.where(core == 0, frame_at > 0, frame_at < lax.axis_size("frame") - 1),
            z_at == 1,
        ]
    ).astype(jnp.float32)
    per_group = 2 * channels // GROUPS

    joined = jnp.stack([enc_feats, skip_feats])
    wide = joined.astype(jnp.float32)
    local = jnp.stack([jnp.sum(wide, axis=(1, 2, 3, 4)), jnp.sum(wide * wide, axis=(1, 2, 3, 4))])

    def by_core(mine, theirs):
        return jnp.where(core == 0, mine, theirs), jnp.where(core == 0, theirs, mine)

    planes = jnp.transpose(joined, (2, 3, 0, 1, 4))
    kept = lax.dynamic_index_in_dim(planes, core, 0, keepdims=False)
    given = lax.dynamic_index_in_dim(planes, 1 - core, 0, keepdims=False)
    partial = jnp.stack(by_core(local, core_swap(local)), axis=2).reshape(2, 4)
    taken = core_swap(given)
    chunk = jnp.concatenate(by_core(kept, taken), axis=2)
    chunk = chunk.reshape(rows, 4 * own_chans, cols)
    before, after = edge_rows(chunk[:1], chunk[rows - 1 :], strip_at % 2 == 0)
    total = sum_over_strips(sum_over(partial, "frame"))
    in_count = frames * rows * cols * spread * per_group
    side = kernel_call(
        functools.partial(side_kernel, count_all=in_count),
        jax.ShapeDtypeStruct((3, 4 * own_chans, cols), jnp.bfloat16),
        (),
        jnp.broadcast_to(total[:, :, None], (2, 4, cols)),
        before,
        after,
        limit=4,
    )

    ahead, behind = (1, -1), (-1, 1)
    z_piece = z_swap(chunk)
    a_piece = from_x(chunk, ahead)
    b_piece = from_x(chunk, behind)
    az_piece = z_swap(a_piece)
    bz_piece = from_x(z_piece, behind)
    d_piece = from_x(a_piece, ahead)
    dz_piece = from_x(bz_piece, behind)
    own_sides = kernel_call(
        pair_kernel,
        jax.ShapeDtypeStruct((2, 3, 4 * own_chans, cols), jnp.bfloat16),
        (),
        side,
        z_swap(side),
        limit=4,
    )
    a_sides = from_x(own_sides, ahead)
    b_sides = from_x(own_sides, behind)
    d_sides = from_x(own_sides, (2, 2))
    width = 2 * channels
    step_word = step_at.astype(jnp.int32)[None]
    core_word = core.astype(jnp.int32)[None]
    second_weight, near_weight = kernel_call(
        second_weights_kernel,
        (
            jax.ShapeDtypeStruct((3 * channels, 3 * channels), jnp.bfloat16),
            jax.ShapeDtypeStruct((2 * channels, 3 * channels), jnp.bfloat16),
        ),
        (2,),
        conv_second.reshape(3, 3 * channels, channels),
        temporal_weight,
        core_word,
        limit=6,
    )

    half_chans = channels // 2
    freq_table = jnp.exp(
        -math.log(10000.0) * jnp.arange(half_chans, dtype=jnp.float32) / half_chans
    )
    angle_rows = timesteps.astype(jnp.float32)[:, None] * freq_table[None, :]
    sinus_rows = jnp.concatenate([jnp.cos(angle_rows), jnp.sin(angle_rows)], axis=1).astype(
        jnp.bfloat16
    )
    wide_one = jnp.dot(sinus_rows, time_first, preferred_element_type=jnp.float32)
    embed_one = jax.nn.silu(wide_one).astype(jnp.bfloat16)
    embed_two = jax.nn.silu(
        jnp.dot(embed_one, time_second, preferred_element_type=jnp.float32)
    ).astype(jnp.bfloat16)
    embed = jnp.dot(embed_two, embed_proj, preferred_element_type=jnp.float32)[0]
    embeds = jnp.stack([embed, core_swap(embed)])
    embed_wide = jnp.broadcast_to(embeds[:, :, None], (2, channels, cols))

    bf16_rows = jax.ShapeDtypeStruct((rows, channels, cols), jnp.bfloat16)
    f32_rows = jax.ShapeDtypeStruct((rows, channels, cols), jnp.float32)
    act, plain = kernel_call(
        norm_kernel,
        (
            jax.ShapeDtypeStruct((rows + 2, width, cols), jnp.float32),
            jax.ShapeDtypeStruct((rows, width, cols), jnp.float32),
        ),
        (0, 1),
        step_word, keep, chunk, z_piece, a_piece, az_piece, b_piece, bz_piece, d_piece, dz_piece,
        own_sides, a_sides, b_sides, d_sides,
        work=4000000000,
        limit=4,
    )
    bf16_rows = jax.ShapeDtypeStruct((rows, channels, cols), jnp.bfloat16)
    conv_own, side_own, sums = kernel_call(
        first_kernel,
        (
            bf16_rows,
            bf16_rows,
            jax.ShapeDtypeStruct((2, 2, GROUPS, cols), jnp.float32),
        ),
        (),
        act, plain, embed_wide, conv_first.reshape(3, 3 * channels, width), skip_weight,
        scratch=(
            pltpu.VMEM(((rows + 1) * width, 256), jnp.bfloat16),
            pltpu.VMEM((rows // 2 * width, 256), jnp.bfloat16),
            pltpu.VMEM((4, channels, cols), jnp.float32),
            pltpu.VMEM((3 * channels, 3 * width), jnp.bfloat16),
            pltpu.SemaphoreType.DMA((3,)),
        ),
        work=4200000000,
        limit=14,
        hbm=(3,),
    )

    mine = sums[0] + core_swap(sums[1])
    mine = sum_over_strips(sum_over(mine, "frame"))
    mid_count = frames * rows * cols * spread * (channels // GROUPS)

    upper = jnp.broadcast_to(keep[3:].reshape(1, 1), (channels, cols)) > 0.5
    beside = link_swap(jnp.where(upper, conv_own[rows - 1], conv_own[0]))
    across = z_swap(beside)
    up = jnp.where(upper, across, beside)
    down = jnp.where(upper, beside, across)
    rims = jnp.stack([up, down])
    conv_other = core_swap(conv_own)
    side_other = core_swap(side_own)
    rims_other = core_swap(rims)

    conv_far = to_next_group(conv_own)
    rims_far = to_next_group(rims)

    def second_conv(conv, rims, outs):
        return kernel_call(
            functools.partial(second_kernel, count_all=mid_count),
            outs,
            (0,),
            keep, conv, rims[0], rims[1], mine, embed_wide, second_weight,
            scratch=(pltpu.VMEM(((rows + 1) * channels, 256), jnp.bfloat16),),
            work=2000000000,
            limit=6,
        )

    f32_rows = jax.ShapeDtypeStruct((rows, channels, cols), jnp.float32)
    second_own, temporal_own = second_conv(conv_own, rims, (f32_rows, bf16_rows))
    other_side = to_frames(temporal_own, (-1, 1))
    second_other, temporal_other = second_conv(conv_other, rims_other, (f32_rows, bf16_rows))
    (temporal_far,) = second_conv(conv_far, rims_far, (bf16_rows,))
    own_block, base = kernel_call(
        near_kernel,
        (jax.ShapeDtypeStruct((channels, rows, cols), jnp.bfloat16), f32_rows),
        (),
        temporal_own, temporal_other, temporal_far, second_own, second_other,
        side_own, side_other, near_weight,
        limit=8,
    )
    decoded = kernel_call(
        far_kernel,
        jax.ShapeDtypeStruct((channels, 2, rows, cols), jnp.bfloat16),
        (0,),
        core_word, other_side, base, own_block, temporal_weight,
        limit=8,
    )
    return decoded[None]


def solution(mesh):
    return jax.shard_map(
        on_device,
        mesh=mesh,
        in_specs=(
            P("step", "frame", "strip", None),
            P("step", "frame", "strip", None),
            P("step"),
            P(),
            P(),
            P(),
            P(),
            P(),
            P(),
            P(),
        ),
        out_specs=P("step", None, "frame", "strip", None),
        check_vma=False,
    )
```
